256 devices in a mesh: gossip: 16 (over z, x_lo), fsdp: 16 (over x_hi, y, core).
Axes of the slice: x: 4 (x_hi: 2, x_lo: 2; x = x_hi * 2 + x_lo), y: 4, z: 8, core: 2. Of those that a mesh axis runs over, the one named last changes fastest.
Arguments:
- inputs: bfloat16 [16, 2048, 2048], P('gossip', 'fsdp'), may hold values from -6 to 6
- out_grad: bfloat16 [16, 2048, 2048], P('gossip', 'fsdp'), may hold values from -6 to 6
- norm_gain: float32 [16, 2048], P('gossip'), may hold values from 0.5 to 1.5
- w_qkv: bfloat16 [16, 16, 2048, 384], P('gossip', 'fsdp'), may hold values from -64 to 64
- w_out: bfloat16 [16, 16, 128, 2048], P('gossip', 'fsdp'), may hold values from -6 to 6
- mom_qkv: bfloat16 [16, 16, 2048, 384], P('gossip', 'fsdp'), may hold values from -6 to 6
- mom_out: bfloat16 [16, 16, 128, 2048], P('gossip', 'fsdp'), may hold values from -6 to 6
- step_index: int32 [1], replicated, may hold values from 0 to 11
Outputs:
- new_qkv: bfloat16 [16, 16, 2048, 384], P('gossip', 'fsdp')
- new_out: bfloat16 [16, 16, 128, 2048], P('gossip', 'fsdp')
- new_mom_qkv: bfloat16 [16, 16, 2048, 384], P('gossip', 'fsdp')
- new_mom_out: bfloat16 [16, 16, 128, 2048], P('gossip', 'fsdp')
The draws below stay inside these ranges and needn't reach their ends.
All inputs are finite; a program needn't handle non-finite values.
Results may differ from the reference program's by a relative error of at most 0.0085.
Values may be sent and summed in bfloat16 or wider, within the bound.
A program may use at most 128 MiB of HBM per device.

```python
import math
import jax
import jax.numpy as jnp
from jax import lax

D = 2048
HEADS = 16
HD = 128
SEQ = 2048
LEVELS = 3
N_GOSSIP = 16


def draw_w_qkv(key, part):
    first_key = jax.random.fold_in(jax.random.fold_in(key, 11), 0)
    base = jnp.clip(jax.random.normal(first_key, (N_GOSSIP, HEADS, D, 3 * HD), jnp.float32), -6.0, 6.0)
    return base.astype(jnp.bfloat16)


def block_levels(key, extent, cuts, least, top_value):
    level, own = 1.0, jax.random.fold_in(key, 6)
    for dim, shards_of in cuts:
        heights = jnp.exp(jax.random.uniform(jax.random.fold_in(own, dim), (shards_of,), jnp.float32, least / len(cuts), top_value / len(cuts)))
        level = level * jnp.repeat(heights, extent[dim] // shards_of).reshape([-1 if axis == dim else 1 for axis in range(len(extent))])
    return level


def gaussian(rng, shape, deviation, limit, cuts=(), held_as=jnp.bfloat16):
    result = deviation * jax.random.normal(rng, shape, jnp.float32)
    if cuts:
        result = result * block_levels(rng, shape, cuts, -0.22, 0.18)
    return jnp.clip(result, -limit, limit).astype(held_as)


def setup_inputs(seed: int = 0) -> dict:
    keys = jax.random.split(jax.random.key(seed), 9)
    return {
        "inputs": gaussian(keys[0], (N_GOSSIP, SEQ, D), 1.0, 6.0, ((0, 16), (1, 16))),
        "out_grad": gaussian(keys[1], (N_GOSSIP, SEQ, D), 1.0, 6.0, ((0, 16), (1, 16))),
        "norm_gain": jnp.clip(1.0 + 0.1 * jax.random.normal(keys[2], (N_GOSSIP, D), jnp.float32), 0.5, 1.5),
        "w_qkv": draw_w_qkv(jax.random.fold_in(keys[8], 71), 0),
        "w_out": gaussian(keys[4], (N_GOSSIP, HEADS, HD, D), 1.0, 6.0, ((0, 16), (1, 16))),
        "mom_qkv": gaussian(keys[5], (N_GOSSIP, HEADS, D, 3 * HD), 1.0, 6.0, ((0, 16), (1, 16))),
        "mom_out": gaussian(keys[6], (N_GOSSIP, HEADS, HD, D), 1.0, 6.0, ((0, 16), (1, 16))),
        "step_index": jax.random.randint(keys[7], (1,), 0, 4 * LEVELS).astype(jnp.int32),
    }


BETA = 0.9
RATE = 0.1
EPSILON = 1e-05

def rotate(tensor, positions):
    half_width = tensor.shape[-1] // 2
    frequency = jnp.exp(-math.log(10000.0) * 2.0 * jnp.arange(half_width, dtype=jnp.float32) / tensor.shape[-1])
    angles = positions.astype(jnp.float32)[:, None] * frequency[None, :]
    cosine = jnp.cos(angles)
    sine_vals = jnp.sin(angles)
    first = tensor[..., :half_width]
    second = tensor[..., half_width:]
    return jnp.concatenate([first * cosine - second * sine_vals, second * cosine + first * sine_vals], -1)

def unrotate(grad_in, positions):
    half_width = grad_in.shape[-1] // 2
    frequency = jnp.exp(-math.log(10000.0) * 2.0 * jnp.arange(half_width, dtype=jnp.float32) / grad_in.shape[-1])
    angles = positions.astype(jnp.float32)[:, None] * frequency[None, :]
    cosine = jnp.cos(angles)
    sine_vals = jnp.sin(angles)
    first = grad_in[..., :half_width]
    second = grad_in[..., half_width:]
    return jnp.concatenate([first * cosine + second * sine_vals, second * cosine - first * sine_vals], -1)

def attend(queries, key_rows, val_rows):
    seq_len, head_dim = queries.shape
    block_len = min(512, seq_len)
    scale = 1.0 / math.sqrt(head_dim)
    outputs = []
    prob_list = []
    for block_num in range(seq_len // block_len):
        begin = block_num * block_len
        key_end = begin + block_len
        scores = jnp.dot(queries[begin:key_end], key_rows[:key_end].T, preferred_element_type=jnp.float32) * scale
        row_pos = begin + jnp.arange(block_len)[:, None]
        col_pos = jnp.arange(key_end)[None, :]
        scores = jnp.where(col_pos <= row_pos, scores, -jnp.inf)
        top = lax.optimization_barrier(jnp.max(scores, -1, keepdims=True))
        weights = jnp.exp(scores - top)
        weights = weights / lax.optimization_barrier(jnp.sum(weights, -1, keepdims=True))
        prob_list.append(weights)
        outputs.append(jnp.dot(weights.astype(jnp.bfloat16), val_rows[:key_end], preferred_element_type=jnp.float32))
    return (jnp.concatenate(outputs, 0).astype(jnp.bfloat16), prob_list)

def attend_back(queries, key_rows, val_rows, prob_list, grad_att):
    seq_len, head_dim = queries.shape
    block_len = min(512, seq_len)
    scale = 1.0 / math.sqrt(head_dim)
    grad_q_list = []
    grad_keys = jnp.zeros((seq_len, head_dim), jnp.float32)
    grad_vals = jnp.zeros((seq_len, head_dim), jnp.float32)
    for block_num in range(seq_len // block_len):
        begin = block_num * block_len
        key_end = begin + block_len
        weights = prob_list[block_num]
        weights_b = weights.astype(jnp.bfloat16)
        grad_block = grad_att[begin:key_end]
        grad_probs = jnp.dot(grad_block, val_rows[:key_end].T, preferred_element_type=jnp.float32)
        centred = grad_probs - lax.optimization_barrier(jnp.sum(weights * grad_probs, -1, keepdims=True))
        grad_scores = (weights * centred * scale).astype(jnp.bfloat16)
        grad_q_list.append(jnp.dot(grad_scores, key_rows[:key_end], preferred_element_type=jnp.float32))
        grad_keys = grad_keys.at[:key_end].add(jnp.dot(grad_scores.T, queries[begin:key_end], preferred_element_type=jnp.float32))
        grad_vals = grad_vals.at[:key_end].add(jnp.dot(weights_b.T, grad_block, preferred_element_type=jnp.float32))
    return (jnp.concatenate(grad_q_list, 0), grad_keys, grad_vals)

def advance(weight, moment, gradient, rate):
    moved_m = (BETA * moment.astype(jnp.float32) + gradient.astype(jnp.float32)).astype(jnp.bfloat16)
    moved_w = (weight.astype(jnp.float32) - rate * moved_m.astype(jnp.float32)).astype(jnp.bfloat16)
    return (moved_w, moved_m)

def replica_update(packed, rate):
    rows, grad_rows, gain_row, weight_qkv, weight_out, moment_qkv, moment_out = packed
    rows_f = rows.astype(jnp.float32)
    stats = lax.rsqrt(lax.optimization_barrier(jnp.mean(rows_f * rows_f, -1, keepdims=True)) + EPSILON)
    normed = (rows_f * stats * gain_row[None, :]).astype(jnp.bfloat16)
    seq_len, width = normed.shape
    head_dim = weight_out.shape[1]
    positions = jnp.arange(seq_len)
    out_scale = 1.0 / math.sqrt(HEADS * head_dim)

    def per_head(head_pair):
        head_qkv, head_out = head_pair
        projected = jnp.dot(normed, head_qkv, preferred_element_type=jnp.float32) * (1.0 / math.sqrt(width))
        queries = rotate(projected[:, :head_dim], positions).astype(jnp.bfloat16)
        key_rows = rotate(projected[:, head_dim:2 * head_dim], positions).astype(jnp.bfloat16)
        val_rows = projected[:, 2 * head_dim:].astype(jnp.bfloat16)
        attended, prob_list = attend(queries, key_rows, val_rows)
        grad_out = (jnp.dot(attended.T, grad_rows, preferred_element_type=jnp.float32) * out_scale).astype(jnp.bfloat16)
        grad_att = (jnp.dot(grad_rows, head_out.T, preferred_element_type=jnp.float32) * out_scale).astype(jnp.bfloat16)
        grad_q, grad_k, grad_v = attend_back(queries, key_rows, val_rows, prob_list, grad_att)
        grad_proj = jnp.concatenate([unrotate(grad_q, positions), unrotate(grad_k, positions), grad_v], -1)
        grad_proj = (grad_proj * (1.0 / math.sqrt(width))).astype(jnp.bfloat16)
        grad_qkv = jnp.dot(normed.T, grad_proj, preferred_element_type=jnp.float32).astype(jnp.bfloat16)
        return (grad_qkv, grad_out)
    grad_qkv, grad_out = lax.map(per_head, (weight_qkv, weight_out))
    moved_qkv, moved_mqkv = advance(weight_qkv, moment_qkv, grad_qkv, rate)
    moved_out, moved_mout = advance(weight_out, moment_out, grad_out, rate)
    return (moved_qkv, moved_out, moved_mqkv, moved_mout)

def reference(inputs, out_grad, norm_gain, w_qkv, w_out, mom_qkv, mom_out, step_index):
    rate = RATE * (step_index[0].astype(jnp.float32) + 1.0) / (4.0 * LEVELS)
    moved = lax.map(lambda packed: replica_update(packed, rate), (inputs, out_grad, norm_gain, w_qkv, w_out, mom_qkv, mom_out))
    exponent = jnp.remainder(step_index[0].astype(jnp.int32), jnp.int32(LEVELS)).astype(jnp.int32)
    distance = jnp.left_shift(jnp.int32(1), exponent)
    results = []
    for own in moved:
        partner = jnp.roll(own, distance, axis=0)
        results.append(((own.astype(jnp.float32) + partner.astype(jnp.float32)) * 0.5).astype(jnp.bfloat16))
    return (results[0], results[1], results[2], results[3])
```

```python
from functools import partial
import math

import jax
import jax.numpy as jnp
from jax import lax
from jax.experimental import pallas as pl
from jax.experimental.pallas import tpu as pltpu
from jax.sharding import PartitionSpec as P

LEVELS = 3
BETA = 0.9
RATE = 0.1
EPSILON = 1e-05
MESH = pl.DeviceIdType.MESH


def rotate(tensor, positions, sign):
    half_width = tensor.shape[-1] // 2
    frequency = jnp.exp(
        -math.log(10000.0) * 2.0 * jnp.arange(half_width, dtype=jnp.float32) / tensor.shape[-1]
    )
    angles = positions.astype(jnp.float32)[:, None] * frequency[None, :]
    cosine = jnp.cos(angles)
    sine_vals = jnp.sin(angles) * sign
    first = tensor[..., :half_width]
    second = tensor[..., half_width:]
    return jnp.concatenate(
        [first * cosine - second * sine_vals, second * cosine + first * sine_vals], -1
    )


def attend(queries, key_rows, val_rows):
    seq_len, head_dim = queries.shape
    block_len = min(512, seq_len)
    scale = 1.0 / math.sqrt(head_dim)
    outputs = []
    prob_list = []
    for block_num in range(seq_len // block_len):
        begin = block_num * block_len
        key_end = begin + block_len
        scores = (
            jnp.dot(
                queries[begin:key_end], key_rows[:key_end].T, preferred_element_type=jnp.float32
            )
            * scale
        )
        row_pos = begin + jnp.arange(block_len)[:, None]
        col_pos = jnp.arange(key_end)[None, :]
        scores = jnp.where(col_pos <= row_pos, scores, -jnp.inf)
        top = jnp.max(scores, -1, keepdims=True)
        weights = jnp.exp(scores - top)
        weights = weights / jnp.sum(weights, -1, keepdims=True)
        prob_list.append(weights)
        outputs.append(
            jnp.dot(
                weights.astype(jnp.bfloat16), val_rows[:key_end], preferred_element_type=jnp.float32
            )
        )
    return (jnp.concatenate(outputs, 0).astype(jnp.bfloat16), prob_list)


def attend_back(queries, key_rows, val_rows, prob_list, grad_att):
    seq_len, head_dim = queries.shape
    block_len = min(512, seq_len)
    scale = 1.0 / math.sqrt(head_dim)
    grad_q_list = []
    grad_keys = jnp.zeros((seq_len, head_dim), jnp.float32)
    grad_vals = jnp.zeros((seq_len, head_dim), jnp.float32)
    for block_num in range(seq_len // block_len):
        begin = block_num * block_len
        key_end = begin + block_len
        weights = prob_list[block_num]
        weights_b = weights.astype(jnp.bfloat16)
        grad_block = grad_att[begin:key_end]
        grad_probs = jnp.dot(grad_block, val_rows[:key_end].T, preferred_element_type=jnp.float32)
        centred = grad_probs - jnp.sum(weights * grad_probs, -1, keepdims=True)
        grad_scores = (weights * centred * scale).astype(jnp.bfloat16)
        grad_q_list.append(
            jnp.dot(grad_scores, key_rows[:key_end], preferred_element_type=jnp.float32)
        )
        grad_keys = grad_keys.at[:key_end].add(
            jnp.dot(grad_scores.T, queries[begin:key_end], preferred_element_type=jnp.float32)
        )
        grad_vals = grad_vals.at[:key_end].add(
            jnp.dot(weights_b.T, grad_block, preferred_element_type=jnp.float32)
        )
    return (jnp.concatenate(grad_q_list, 0), grad_keys, grad_vals)


def move(weight, moved_m, rate):
    return (weight.astype(jnp.float32) - rate * moved_m.astype(jnp.float32)).astype(jnp.bfloat16)


def average(own, other):
    return ((own.astype(jnp.float32) + other.astype(jnp.float32)) * 0.5).astype(jnp.bfloat16)


def greet(targets):
    barrier = pltpu.get_barrier_semaphore()
    for target in targets:
        pl.semaphore_signal(barrier, inc=1, device_id=target, device_id_type=MESH)
    pl.semaphore_wait(barrier, len(targets))


def gather_kernel(by, x_ref, og_ref, wq_ref, wo_ref, ax_ref, aog_ref, pq_ref, po_ref,
                  send_sem, recv_sem, loc_sem):
    g = lax.axis_index("gossip")
    f = lax.axis_index("fsdp")
    core = lax.rem(f, 2)
    y = lax.rem(f // 2, 4)
    xh = f // 8
    n_g = lax.axis_size("gossip")

    def dev(xx, yy, cc):
        return xx * 8 + lax.rem(yy + 4, 4) * 2 + cc

    up = (g, dev(xh, y + 1, core))
    down = (g, dev(xh, y - 1, core))
    sib = (g, dev(xh, y, 1 - core))
    across = (g, dev(1 - xh, y, core))
    partner = (lax.rem(g + by, n_g), f)
    source = (lax.rem(g - by + n_g, n_g), f)
    greet([up, down, sib, across, partner, source])

    def slot(xx, yy):
        return dev(xx, yy, core)

    counter = [0]

    def send(src, dst, target):
        i = counter[0]
        counter[0] += 1
        return pltpu.make_async_remote_copy(
            src_ref=src, dst_ref=dst, send_sem=send_sem.at[i], recv_sem=recv_sem.at[i],
            device_id=target, device_id_type=MESH)

    arrays = ((x_ref, ax_ref), (og_ref, aog_ref))
    copies = []
    local = []
    first = []
    for a, (src, dst) in enumerate(arrays):
        mine = slot(xh, y)
        own = src.at[0]
        lc = pltpu.make_async_copy(own, dst.at[mine], loc_sem.at[a])
        local.append(lc)
        c = dict(up=send(own, dst.at[mine], up), down=send(own, dst.at[mine], down),
                 across=send(own, dst.at[mine], across), sib=send(own, dst.at[mine], sib))
        first.append(c)
    for c in first[:1]:
        for k in ("up", "down", "across", "sib"):
            c[k].start()
    first[1]["across"].start()
    half = 64

    def ring_rest(a, side, c):
        dst = arrays[a][1]
        lo = dst.at[slot(side, y - 1)]
        hi = dst.at[slot(side, y + 1)]
        c["up"].wait_recv()
        u2 = send(lo.at[pl.ds(0, half)], lo.at[pl.ds(0, half)], up)
        s1 = send(lo, lo, sib)
        u2.start()
        s1.start()
        c["down"].wait_recv()
        d2 = send(hi.at[pl.ds(half, half)], hi.at[pl.ds(half, half)], down)
        s2 = send(hi, hi, sib)
        d2.start()
        s2.start()
        return u2, d2, s1, s2

    def ring_last(a, side, u2, d2):
        dst = arrays[a][1]
        far = dst.at[slot(side, y + 2)]
        u2.wait_recv()
        s3 = send(far.at[pl.ds(0, half)], far.at[pl.ds(0, half)], sib)
        s3.start()
        d2.wait_recv()
        s4 = send(far.at[pl.ds(half, half)], far.at[pl.ds(half, half)], sib)
        s4.start()
        return s3, s4

    def second(a, c):
        dst = arrays[a][1]
        row = dst.at[slot(1 - xh, y)]
        c["across"].wait_recv()
        c2 = dict(up=send(row, row, up), down=send(row, row, down), sib=send(row, row, sib))
        for k in ("up", "down", "sib"):
            c2[k].start()
        return c2

    done_recv = []
    sends = []
    wq = send(wq_ref, pq_ref, partner)
    wo = send(wo_ref, po_ref, partner)

    r1 = ring_rest(0, xh, first[0])
    c2 = second(0, first[0])
    for k in ("up", "down", "sib"):
        first[1][k].start()
    l1 = ring_last(0, xh, r1[0], r1[1])
    r2 = ring_rest(0, 1 - xh, c2)
    r3 = ring_rest(1, xh, first[1])
    c4 = second(1, first[1])
    wq.start()
    wo.start()
    for lc in local:
        lc.start()
    l2 = ring_last(0, 1 - xh, r2[0], r2[1])
    l3 = ring_last(1, xh, r3[0], r3[1])
    r4 = ring_rest(1, 1 - xh, c4)
    l4 = ring_last(1, 1 - xh, r4[0], r4[1])

    sib_copies = [first[0]["sib"], first[1]["sib"], c2["sib"], c4["sib"]]
    for r in (r1, r2, r3, r4):
        sib_copies += [r[2], r[3]]
    for l in (l1, l2, l3, l4):
        sib_copies += list(l)
    for c in sib_copies:
        c.wait_recv()
        c.wait_send()
    for c in first:
        for k in ("up", "down", "across"):
            c[k].wait_send()
    for c in (c2, c4):
        c["up"].wait_send()
        c["down"].wait_send()
    for r in (r1, r2, r3, r4):
        r[0].wait_send()
        r[1].wait_send()
    for lc in local:
        lc.wait()
    wq.wait()
    wo.wait()


N_COPIES = 40


def gather(by, cid, x, og, wq, wo):
    seq = x.shape[1] * lax.axis_size("fsdp")
    rows, width = x.shape[1:]
    slots = seq // rows
    anyspec = pl.BlockSpec(memory_space=pl.ANY)
    return pl.pallas_call(
        partial(gather_kernel, by),
        out_shape=(
            jax.ShapeDtypeStruct((slots, rows, width), jnp.bfloat16),
            jax.ShapeDtypeStruct((slots, rows, width), jnp.bfloat16),
            jax.ShapeDtypeStruct(wq.shape, jnp.bfloat16),
            jax.ShapeDtypeStruct(wo.shape, jnp.bfloat16),
        ),
        in_specs=[anyspec] * 4,
        out_specs=[anyspec] * 4,
        scratch_shapes=[
            pltpu.SemaphoreType.DMA((N_COPIES,)),
            pltpu.SemaphoreType.DMA((N_COPIES,)),
            pltpu.SemaphoreType.DMA((2,)),
        ],
        name=f"gather_{by}",
        compiler_params=pltpu.CompilerParams(collective_id=cid, has_side_effects=True),
    )(x, og, wq, wo)


def push_kernel(by, mq_ref, mo_ref, pq_ref, po_ref, send_sem, recv_sem):
    g = lax.axis_index("gossip")
    f = lax.axis_index("fsdp")
    n_g = lax.axis_size("gossip")
    partner = (lax.rem(g + by, n_g), f)
    source = (lax.rem(g - by + n_g, n_g), f)
    barrier = pltpu.get_barrier_semaphore()
    pl.semaphore_signal(barrier, inc=1, device_id=source, device_id_type=MESH)
    pl.semaphore_wait(barrier, 1)
    copies = []
    for i, (src, dst) in enumerate(((mq_ref, pq_ref), (mo_ref, po_ref))):
        copies.append(pltpu.make_async_remote_copy(
            src_ref=src, dst_ref=dst, send_sem=send_sem.at[i], recv_sem=recv_sem.at[i],
            device_id=partner, device_id_type=MESH))
        copies[-1].start()
    for c in copies:
        c.wait()


def push(by, cid, mq, mo):
    anyspec = pl.BlockSpec(memory_space=pl.ANY)
    return pl.pallas_call(
        partial(push_kernel, by),
        out_shape=(
            jax.ShapeDtypeStruct(mq.shape, jnp.bfloat16),
            jax.ShapeDtypeStruct(mo.shape, jnp.bfloat16),
        ),
        in_specs=[anyspec] * 2,
        out_specs=[anyspec] * 2,
        scratch_shapes=[pltpu.SemaphoreType.DMA((2,)), pltpu.SemaphoreType.DMA((2,))],
        name=f"push_{by}",
        compiler_params=pltpu.CompilerParams(collective_id=cid, has_side_effects=True),
    )(mq, mo)


def per_device(inputs, out_grad, norm_gain, w_qkv, w_out, mom_qkv, mom_out, step_index):
    rate = RATE * (step_index[0].astype(jnp.float32) + 1.0) / (4.0 * LEVELS)
    exponent = jnp.remainder(step_index[0], LEVELS)
    all_x, piece, other_wq, other_wo = lax.switch(
        exponent, [partial(gather, 1 << k, k) for k in range(LEVELS)],
        inputs, out_grad, w_qkv, w_out)
    width = all_x.shape[-1]
    rows_f = all_x.reshape(-1, width).astype(jnp.float32)
    piece = piece.reshape(-1, width)
    stats = lax.rsqrt(jnp.mean(rows_f * rows_f, -1, keepdims=True) + EPSILON)
    all_normed = (rows_f * stats * norm_gain[0][None, :]).astype(jnp.bfloat16)
    seq_len = all_normed.shape[0]
    head_qkv = w_qkv[0, 0]
    head_out = w_out[0, 0]
    head_dim = head_out.shape[0]
    positions = jnp.arange(seq_len)
    out_scale = 1.0 / math.sqrt(lax.axis_size("fsdp") * head_dim)
    projected = jnp.dot(all_normed, head_qkv, preferred_element_type=jnp.float32) * (
        1.0 / math.sqrt(width))
    queries = rotate(projected[..., :head_dim], positions, 1.0).astype(jnp.bfloat16)
    key_rows = rotate(projected[..., head_dim: 2 * head_dim], positions, 1.0).astype(jnp.bfloat16)
    val_rows = projected[..., 2 * head_dim:].astype(jnp.bfloat16)
    attended, prob_list = attend(queries, key_rows, val_rows)
    grad_out = (jnp.dot(attended.T, piece, preferred_element_type=jnp.float32)
                * out_scale).astype(jnp.bfloat16)
    grad_att = (jnp.dot(piece, head_out.T, preferred_element_type=jnp.float32)
                * out_scale).astype(jnp.bfloat16)
    grad_q, grad_k, grad_v = attend_back(queries, key_rows, val_rows, prob_list, grad_att)
    grad_proj = jnp.concatenate(
        [rotate(grad_q, positions, -1.0), rotate(grad_k, positions, -1.0), grad_v], -1)
    grad_proj = (grad_proj * (1.0 / math.sqrt(width))).astype(jnp.bfloat16)
    grad_qkv = jnp.dot(all_normed.T, grad_proj,
                       preferred_element_type=jnp.float32).astype(jnp.bfloat16)
    mm_q = (BETA * mom_qkv.astype(jnp.float32) + grad_qkv.astype(jnp.float32)).astype(jnp.bfloat16)
    mm_o = (BETA * mom_out.astype(jnp.float32) + grad_out.astype(jnp.float32)).astype(jnp.bfloat16)
    other_mq, other_mo = lax.switch(
        exponent, [partial(push, 1 << k, LEVELS + k) for k in range(LEVELS)], mm_q, mm_o)
    return (
        average(move(w_qkv, mm_q, rate), move(other_wq, other_mq, rate)),
        average(move(w_out, mm_o, rate), move(other_wo, other_mo, rate)),
        average(mm_q, other_mq),
        average(mm_o, other_mo),
    )


def solution(mesh):
    return jax.shard_map(
        per_device,
        mesh=mesh,
        in_specs=(
            P("gossip", "fsdp", None),
            P("gossip", "fsdp", None),
            P("gossip", None),
            P("gossip", "fsdp", None, None),
            P("gossip", "fsdp", None, None),
            P("gossip", "fsdp", None, None),
            P("gossip", "fsdp", None, None),
            P(),
        ),
        out_specs=(
            P("gossip", "fsdp", None, None),
            P("gossip", "fsdp", None, None),
            P("gossip", "fsdp", None, None),
            P("gossip", "fsdp", None, None),
        ),
        check_vma=False,
    )
```

```python
from functools import partial
import math

import jax
import jax.numpy as jnp
from jax import lax
from jax.experimental import pallas as pl
from jax.experimental.pallas import tpu as pltpu
from jax.sharding import PartitionSpec as P

LEVELS = 3
BETA = 0.9
RATE = 0.1
EPSILON = 1e-05
MESH = pl.DeviceIdType.MESH
F32 = jnp.float32
BF16 = jnp.bfloat16

(UP, DOWN, ACROSS, SIB, U2, D2, S_LO, S_HI, C_UP, C_DOWN, C_SIB, AX1, AX2, S_F1, S_F2,
 S_OLO, S_OHI, S_OF1, S_OF2) = range(19)
PER_ARRAY = 19
WQ = 2 * PER_ARRAY
WO = WQ + 1
MO = WQ + 2
MQ = WQ + 3


def dot_nt(a, b):
    return lax.dot_general(a, b, (((1,), (1,)), ((), ())), preferred_element_type=F32)


def dot_tn(a, b):
    return lax.dot_general(a, b, (((0,), (0,)), ((), ())), preferred_element_type=F32)


def pick(i, values):
    out = jnp.int32(values[0])
    for k in range(1, len(values)):
        out = jnp.where(i == k, jnp.int32(values[k]), out)
    return out


def average(own, other):
    return ((own.astype(F32) + other.astype(F32)) * 0.5).astype(BF16)


def move(weight, moved_m, rate):
    return (weight.astype(F32) - rate * moved_m.astype(F32)).astype(BF16)


def kernel(by, rate_ref, gain_ref, hc_ref, hs_ref, lc_ref, ls_ref,
           x_ref, og_ref, wq_ref, wo_ref, mq_ref, mo_ref,
           nwq_ref, nwo_ref, nmq_ref, nmo_ref,
           ax, aog, n_t, n_tmp, wq_v, wo_v, mq_v, mo_v, pq_v, po_v, rq_v, ro_v,
           q_s, k_s, v_s, att_t, o_s, s_s, p_s, go_s, dk_s, dv_s, gp_s,
           send_sem, recv_sem, loc_sem):
    g = lax.axis_index("gossip")
    f = lax.axis_index("fsdp")
    n_g = lax.axis_size("gossip")
    core = lax.rem(f, 2)
    y = lax.rem(f // 2, 4)
    xh = f // 8
    chunks, block, width = ax.shape
    rows = block // 2
    half = rows // 2
    head_dim = wo_v.shape[0]
    out_scale = 1.0 / math.sqrt(lax.axis_size("fsdp") * head_dim)
    in_scale = 1.0 / math.sqrt(width)
    scale = 1.0 / math.sqrt(head_dim)

    def dev(xx, yy, cc):
        return xx * 8 + lax.rem(yy + 4, 4) * 2 + cc

    up = (g, dev(xh, y + 1, core))
    down = (g, dev(xh, y - 1, core))
    sib = (g, dev(xh, y, 1 - core))
    across = (g, dev(1 - xh, y, core))
    partner = (lax.rem(g + by, n_g), f)
    source = (lax.rem(g - by + n_g, n_g), f)

    def chunk(side, yy):
        return side * 4 + lax.rem(yy + 4, 4)

    def piece(dst, side, yy, part=None):
        first = pl.multiple_of(core * rows, rows)
        if part is None:
            return dst.at[chunk(side, yy), pl.ds(first, rows)]
        return dst.at[chunk(side, yy), pl.ds(pl.multiple_of(first + part * half, half), half)]

    def remote(i, src, dst, target):
        return pltpu.make_async_remote_copy(
            src_ref=src, dst_ref=dst, send_sem=send_sem.at[i], recv_sem=recv_sem.at[i],
            device_id=target, device_id_type=MESH)

    arrays = ((x_ref, ax), (og_ref, aog))

    def copy(a, i):
        src, dst = arrays[a]
        own, other = xh, 1 - xh
        n = a * PER_ARRAY + i

        def same(where, target):
            return remote(n, where, where, target)

        if i in (UP, DOWN, ACROSS, SIB):
            return remote(n, src.at[0], piece(dst, own, y),
                          {UP: up, DOWN: down, ACROSS: across, SIB: sib}[i])
        if i == U2:
            return same(piece(dst, own, y - 1, 0), up)
        if i == D2:
            return same(piece(dst, own, y + 1, 1), down)
        if i == S_LO:
            return same(piece(dst, own, y - 1), sib)
        if i == S_HI:
            return same(piece(dst, own, y + 1), sib)
        if i in (C_UP, C_DOWN, C_SIB):
            return same(piece(dst, other, y), {C_UP: up, C_DOWN: down, C_SIB: sib}[i])
        if i == AX1:
            return same(piece(dst, own, y + 2, 0), across)
        if i == AX2:
            return same(piece(dst, own, y + 2, 1), across)
        if i == S_F1:
            return same(piece(dst, own, y + 2, 0), sib)
        if i == S_F2:
            return same(piece(dst, own, y + 2, 1), sib)
        if i == S_OLO:
            return same(piece(dst, other, y - 1), sib)
        if i == S_OHI:
            return same(piece(dst, other, y + 1), sib)
        if i == S_OF1:
            return same(piece(dst, other, y + 2, 0), sib)
        return same(piece(dst, other, y + 2, 1), sib)

    def start(a, *which):
        for i in which:
            copy(a, i).start()

    def arrived(a, *which):
        for i in which:
            copy(a, i).wait_recv()

    def local(i, src, dst):
        return pltpu.make_async_copy(src, dst, loc_sem.at[i])

    def own_copy(a):
        return local(a, arrays[a][0].at[0], piece(arrays[a][1], xh, y))

    loads = [local(2, wq_ref, wq_v), local(3, wo_ref, wo_v),
             local(4, mq_ref, mq_v), local(5, mo_ref, mo_v)]
    send_wq = remote(WQ, wq_ref, pq_v, partner)
    send_wo = remote(WO, wo_ref, po_v, partner)
    send_mo = remote(MO, mo_v, ro_v, partner)

    def send_mq(d):
        at = pl.ds(pl.multiple_of(d * block, block), block)
        return remote(MQ + d, mq_v.at[at], rq_v.at[at], partner)

    own_copy(0).start()
    loads[0].start()
    barrier = pltpu.get_barrier_semaphore()
    everyone = [up, down, sib, across, partner, source]
    for target in everyone:
        pl.semaphore_signal(barrier, inc=1, device_id=target, device_id_type=MESH)
    pl.semaphore_wait(barrier, len(everyone))
    start(0, UP, DOWN, ACROSS, SIB)
    own_copy(1).start()
    for c in loads[1:]:
        c.start()
    loads[0].wait()

    def near(a):
        arrived(a, UP)
        start(a, U2, S_LO)
        arrived(a, DOWN)
        start(a, D2, S_HI)

    def row(a):
        arrived(a, ACROSS)
        start(a, C_UP, C_DOWN, C_SIB)

    def far(a):
        arrived(a, U2)
        start(a, AX1, S_F1)
        arrived(a, D2)
        start(a, AX2, S_F2)

    def other_near(a):
        arrived(a, C_UP)
        start(a, S_OLO)
        arrived(a, C_DOWN)
        start(a, S_OHI)

    def other_far(a):
        arrived(a, AX1)
        start(a, S_OF1)
        arrived(a, AX2)
        start(a, S_OF2)

    def when(i, k, *steps):
        @pl.when(i == k)
        def _():
            for s in steps:
                s()

    def chunk_at(i):
        side = pick(i, (0, 0, 0, 1, 0, 1, 1, 1))
        move_y = pick(i, (0, 3, 1, 0, 2, 3, 1, 2))
        return lax.rem(xh + side, 2) * 4 + lax.rem(y + move_y, 4)

    def tables(m):
        hc, hs = hc_ref[pl.ds(m, 1), :], hs_ref[pl.ds(m, 1), :]
        lc, ls = lc_ref[...], ls_ref[...]
        return hc * lc - hs * ls, hs * lc + hc * ls

    def turned(t):
        return pltpu.roll(t, head_dim // 2, 1)

    def project(i, _):
        when(i, 0, lambda: own_copy(0).wait(), lambda: arrived(0, SIB))
        when(i, 1, lambda: near(0), lambda: row(0), lambda: start(1, ACROSS),
             lambda: arrived(0, S_LO))
        when(i, 2, lambda: arrived(0, S_HI))
        when(i, 3, lambda: far(0), lambda: start(1, UP, DOWN, SIB), send_wq.start,
             send_wo.start, lambda: arrived(0, C_SIB))
        when(i, 4, lambda: arrived(0, S_F1, S_F2))
        when(i, 5, lambda: other_near(0), lambda: row(1), lambda: arrived(0, S_OLO))
        when(i, 6, lambda: other_far(0), lambda: arrived(0, S_OHI))
        when(i, 7, lambda: arrived(0, S_OF1, S_OF2))
        m = chunk_at(i)

        def norm(r, _):
            at = pl.ds(pl.multiple_of(r * 32, 32), 32)
            t = ax[m, at, :].astype(F32)
            stats = lax.rsqrt(jnp.mean(t * t, -1, keepdims=True) + EPSILON)
            n_tmp[at, :] = (t * stats * gain_ref[...]).astype(BF16)
            return 0

        lax.fori_loop(0, block // 32, norm, 0)

        def flip(c, _):
            at = pl.ds(pl.multiple_of(c * block, block), block)
            n_t[m, at, :] = n_tmp[:, at].T
            return 0

        lax.fori_loop(0, width // block, flip, 0)
        proj = jnp.dot(n_tmp[...], wq_v[...], preferred_element_type=F32) * in_scale
        cos, sin = tables(m)
        q = proj[:, :head_dim]
        k = proj[:, head_dim:2 * head_dim]
        q_s[m] = (q * cos + turned(q) * sin).astype(BF16)
        k_s[m] = (k * cos + turned(k) * sin).astype(BF16)
        v_s[m] = proj[:, 2 * head_dim:].astype(BF16)
        dk_s[m] = jnp.zeros_like(dk_s[m])
        dv_s[m] = jnp.zeros_like(dv_s[m])
        return 0

    lax.fori_loop(0, chunks, project, 0)

    row_pos = lax.broadcasted_iota(jnp.int32, (block, block), 0)
    col_pos = lax.broadcasted_iota(jnp.int32, (block, block), 1)

    def folded(t, op):
        return op(t[:, :head_dim], t[:, head_dim:])

    def forward(m, _):
        when(m, 0, lambda: near(1))
        when(m, 4, lambda: far(1))
        when(m, 7, lambda: other_near(1))
        q = q_s[m]

        def scores(j, top):
            s = dot_nt(q, k_s[j]) * scale
            s = jnp.where(col_pos + j * block <= row_pos + m * block, s, -jnp.inf)
            s_s[j] = s
            return jnp.maximum(top, folded(s, jnp.maximum))

        top = lax.fori_loop(0, m + 1, scores, jnp.full((block, head_dim), -jnp.inf, F32))
        top = jnp.max(top, -1, keepdims=True)

        def exps(j, total):
            e = jnp.exp(s_s[j] - top)
            s_s[j] = e
            return total + folded(e, jnp.add)

        total = lax.fori_loop(0, m + 1, exps, jnp.zeros((block, head_dim), F32))
        inverse = 1.0 / jnp.sum(total, -1, keepdims=True)

        def values(j, out):
            p = (s_s[j] * inverse).astype(BF16)
            p_s[m, j] = p
            return out + jnp.dot(p, v_s[j], preferred_element_type=F32)

        out = lax.fori_loop(0, m + 1, values, jnp.zeros((block, head_dim), F32))
        o_s[m] = out
        att_t[m] = out.astype(BF16).T
        return 0

    lax.fori_loop(0, chunks, forward, 0)
    for c in loads[1:]:
        c.wait()
    go_s[...] = jnp.zeros_like(go_s)

    def backward(i, _):
        when(i, 0, lambda: own_copy(1).wait(), lambda: arrived(1, SIB))
        when(i, 1, lambda: arrived(1, S_LO))
        when(i, 2, lambda: arrived(1, S_HI))
        when(i, 3, lambda: arrived(1, C_SIB))
        when(i, 4, lambda: arrived(1, S_F1, S_F2), lambda: other_far(1))
        when(i, 5, lambda: arrived(1, S_OLO))
        when(i, 6, lambda: arrived(1, S_OHI))
        when(i, 7, lambda: arrived(1, S_OF1, S_OF2))
        m = chunk_at(i)
        da_f = dot_nt(aog[m], wo_v[...]) * out_scale
        da = da_f.astype(BF16)
        go_s[...] += jnp.dot(att_t[m], aog[m], preferred_element_type=F32)

        @pl.when(i == chunks - 1)
        def _():
            def moved(r, _):
                at = pl.ds(pl.multiple_of(r * 16, 16), 16)
                grad = (go_s[at, :] * out_scale).astype(BF16)
                mo_v[at, :] = (BETA * mo_v[at, :].astype(F32) + grad.astype(F32)).astype(BF16)
                return 0

            lax.fori_loop(0, head_dim // 16, moved, 0)
            send_mo.start()

        centre = jnp.sum(da.astype(F32) * o_s[m], -1, keepdims=True)
        q = q_s[m]

        def pair(j, dq):
            p = p_s[m, j]
            ds = (p.astype(F32) * (dot_nt(da, v_s[j]) - centre) * scale).astype(BF16)
            dk_s[j] += dot_tn(ds, q)
            dv_s[j] += dot_tn(p, da)
            return dq + jnp.dot(ds, k_s[j], preferred_element_type=F32)

        dq = lax.fori_loop(0, m + 1, pair, jnp.zeros((block, head_dim), F32))
        cos, sin = tables(m)
        gp_s[m, :, :head_dim] = ((dq * cos - turned(dq) * sin) * in_scale).astype(BF16)
        return 0

    lax.fori_loop(0, chunks, backward, 0)

    def finish(m, _):
        cos, sin = tables(m)
        dk = dk_s[m]
        gp_s[m, :, head_dim:2 * head_dim] = (
            (dk * cos - turned(dk) * sin) * in_scale).astype(BF16)
        gp_s[m, :, 2 * head_dim:] = (dv_s[m] * in_scale).astype(BF16)
        return 0

    lax.fori_loop(0, chunks, finish, 0)

    def grads(d, _):
        at = pl.ds(pl.multiple_of(d * block, block), block)
        total = jnp.dot(n_t[0, at, :], gp_s[0], preferred_element_type=F32)
        for m in range(1, chunks):
            total = total + jnp.dot(n_t[m, at, :], gp_s[m], preferred_element_type=F32)
        mq_v[at, :] = (BETA * mq_v[at, :].astype(F32)
                       + total.astype(BF16).astype(F32)).astype(BF16)
        send_mq(d).start()
        return 0

    lax.fori_loop(0, width // block, grads, 0)
    rate = rate_ref[0]
    send_wq.wait()
    send_wo.wait()
    send_mo.wait()

    def outs_o(r, _):
        at = pl.ds(pl.multiple_of(r * 16, 16), 16)
        mine, theirs = mo_v[at, :], ro_v[at, :]
        nmo_ref[at, :] = average(mine, theirs)
        nwo_ref[at, :] = average(move(wo_v[at, :], mine, rate), move(po_v[at, :], theirs, rate))
        return 0

    lax.fori_loop(0, head_dim // 16, outs_o, 0)

    def outs_q(d, _):
        send_mq(d).wait()
        at = pl.ds(pl.multiple_of(d * block, block), block)
        mine, theirs = mq_v[at, :], rq_v[at, :]
        nmq_ref[at, :] = average(mine, theirs)
        nwq_ref[at, :] = average(move(wq_v[at, :], mine, rate), move(pq_v[at, :], theirs, rate))
        return 0

    lax.fori_loop(0, width // block, outs_q, 0)
    for a in range(2):
        for i in range(PER_ARRAY):
            copy(a, i).wait_send()


def update(by, cid, rate, gain, tables, x, og, wq, wo, mq, mo):
    devices = lax.axis_size("fsdp")
    rows, width = x.shape[1:]
    block = 2 * rows
    chunks = devices // 2
    wide, head_dim = wq.shape[1], wo.shape[0]
    hbm = pl.BlockSpec(memory_space=pl.ANY)
    vmem = pl.BlockSpec(memory_space=pltpu.VMEM)
    n_copies = MQ + width // block

    def v(*shape, dtype=BF16):
        return pltpu.VMEM(shape, dtype)

    return pl.pallas_call(
        partial(kernel, by),
        out_shape=(
            jax.ShapeDtypeStruct(wq.shape, BF16), jax.ShapeDtypeStruct(wo.shape, BF16),
            jax.ShapeDtypeStruct(wq.shape, BF16), jax.ShapeDtypeStruct(wo.shape, BF16),
        ),
        in_specs=[pl.BlockSpec(memory_space=pltpu.SMEM)] + [vmem] * 5 + [hbm] * 6,
        out_specs=[vmem] * 4,
        scratch_shapes=[
            v(chunks, block, width), v(chunks, block, width), v(chunks, width, block),
            v(block, width),
            v(width, wide), v(head_dim, width), v(width, wide), v(head_dim, width),
            v(width, wide), v(head_dim, width), v(width, wide), v(head_dim, width),
            v(chunks, block, head_dim), v(chunks, block, head_dim), v(chunks, block, head_dim),
            v(chunks, head_dim, block), v(chunks, block, head_dim, dtype=F32),
            v(chunks, block, block, dtype=F32), v(chunks, chunks, block, block),
            v(head_dim, width, dtype=F32),
            v(chunks, block, head_dim, dtype=F32), v(chunks, block, head_dim, dtype=F32),
            v(chunks, block, wide),
            pltpu.SemaphoreType.DMA((n_copies,)), pltpu.SemaphoreType.DMA((n_copies,)),
            pltpu.SemaphoreType.DMA((6,)),
        ],
        name=f"update_{by}",
        compiler_params=pltpu.CompilerParams(
            collective_id=cid, has_side_effects=True, vmem_limit_bytes=66_000_000),
    )(rate, gain, *tables, x, og, wq, wo, mq, mo)


def per_device(inputs, out_grad, norm_gain, w_qkv, w_out, mom_qkv, mom_out, step_index):
    rate = RATE * (step_index.astype(F32) + 1.0) / (4.0 * LEVELS)
    exponent = jnp.remainder(step_index[0], LEVELS)
    head_dim = w_out.shape[2]
    rows = inputs.shape[1]
    block, chunks = 2 * rows, lax.axis_size("fsdp") // 2
    half_width = head_dim // 2
    frequency = jnp.exp(
        -math.log(10000.0) * 2.0 * jnp.arange(half_width, dtype=F32) / head_dim)
    frequency = jnp.concatenate([frequency, frequency])
    high = (jnp.arange(chunks) * block).astype(F32)[:, None] * frequency[None, :]
    low = jnp.arange(block).astype(F32)[:, None] * frequency[None, :]
    sign = jnp.where(jnp.arange(head_dim) < half_width, -1.0, 1.0).astype(F32)
    tables = (jnp.cos(high), jnp.sin(high) * sign, jnp.cos(low), jnp.sin(low) * sign)
    outs = lax.switch(
        exponent, [partial(update, 1 << k, k) for k in range(LEVELS)],
        rate, norm_gain, tables, inputs, out_grad,
        w_qkv[0, 0], w_out[0, 0], mom_qkv[0, 0], mom_out[0, 0])
    return tuple(o[None, None] for o in outs)


def solution(mesh):
    return jax.shard_map(
        per_device,
        mesh=mesh,
        in_specs=(
            P("gossip", "fsdp", None),
            P("gossip", "fsdp", None),
            P("gossip", None),
            P("gossip", "fsdp", None, None),
            P("gossip", "fsdp", None, None),
            P("gossip", "fsdp", None, None),
            P("gossip", "fsdp", None, None),
            P(),
        ),
        out_specs=(
            P("gossip", "fsdp", None, None),
            P("gossip", "fsdp", None, None),
            P("gossip", "fsdp", None, None),
            P("gossip", "fsdp", None, None),
        ),
        check_vma=False,
    )
```

```python
from functools import partial
import math

import jax
import jax.numpy as jnp
from jax import lax
from jax.experimental import pallas as pl
from jax.experimental.pallas import tpu as pltpu
from jax.sharding import PartitionSpec as P

LEVELS = 3
BETA = 0.9
RATE = 0.1
EPSILON = 1e-05
MESH = pl.DeviceIdType.MESH
F32 = jnp.float32
BF16 = jnp.bfloat16

(UP, DOWN, ACROSS, SIB, U2, D2, S_LO, S_HI, C_UP, C_DOWN, C_SIB, AX1, AX2, S_F1, S_F2,
 S_OLO, S_OHI, S_OF1, S_OF2) = range(19)
PER_ARRAY = 19
WQ = 2 * PER_ARRAY
WO = WQ + 1
MO = WQ + 2
WO2 = WQ + 3
MO2 = WQ + 4
MQ = WQ + 5


def dot_nt(a, b):
    return lax.dot_general(a, b, (((1,), (1,)), ((), ())), preferred_element_type=F32)


def dot_tn(a, b):
    return lax.dot_general(a, b, (((0,), (0,)), ((), ())), preferred_element_type=F32)


def pick(i, values):
    out = jnp.int32(values[0])
    for k in range(1, len(values)):
        out = jnp.where(i == k, jnp.int32(values[k]), out)
    return out


def average(own, other):
    return ((own.astype(F32) + other.astype(F32)) * 0.5).astype(BF16)


def move(weight, moved_m, rate):
    return (weight.astype(F32) - rate * moved_m.astype(F32)).astype(BF16)


def kernel(by, rate_ref, gain_ref, hc_ref, hs_ref, lc_ref, ls_ref,
           x_ref, og_ref, wq_ref, wo_ref, mq_ref, mo_ref,
           nwq_ref, nwo_ref, nmq_ref, nmo_ref,
           ax, aog, n_s, wrel, mrel, wq_v, wo_v, mq_v, mo_v, pq_v, po_v, rq_v, ro_v,
           q_s, k_s, v_s, qt_s, kt_s, vt_s, att_t, o_s, s_s, p_s, go_s, dk_s, dv_s, gp_s,
           send_sem, recv_sem, loc_sem):
    g = lax.axis_index("gossip")
    f = lax.axis_index("fsdp")
    n_g = lax.axis_size("gossip")
    core = lax.rem(f, 2)
    y = lax.rem(f // 2, 4)
    xh = f // 8
    chunks, block, width = ax.shape
    rows = block // 2
    half = rows // 2
    head_dim = wo_v.shape[0]
    out_scale = 1.0 / math.sqrt(lax.axis_size("fsdp") * head_dim)
    in_scale = 1.0 / math.sqrt(width)
    scale = 1.0 / math.sqrt(head_dim)

    def dev(xx, yy, cc):
        return xx * 8 + lax.rem(yy + 4, 4) * 2 + cc

    up = (g, dev(xh, y + 1, core))
    down = (g, dev(xh, y - 1, core))
    sib = (g, dev(xh, y, 1 - core))
    across = (g, dev(1 - xh, y, core))
    partner = (lax.rem(g + by, n_g), f)
    source = (lax.rem(g - by + n_g, n_g), f)
    leg = 6
    relayed = n_g - by == 2 * leg
    ahead = (lax.rem(g - leg + n_g, n_g), f)
    behind = (lax.rem(g + leg, n_g), f)
    along_y = by == 1

    def chunk(side, yy):
        return side * 4 + lax.rem(yy + 4, 4)

    def piece(dst, side, yy, part=None):
        first = pl.multiple_of(core * rows, rows)
        if part is None:
            return dst.at[chunk(side, yy), pl.ds(first, rows)]
        return dst.at[chunk(side, yy), pl.ds(pl.multiple_of(first + part * half, half), half)]

    def remote(i, src, dst, target):
        return pltpu.make_async_remote_copy(
            src_ref=src, dst_ref=dst, send_sem=send_sem.at[i], recv_sem=recv_sem.at[i],
            device_id=target, device_id_type=MESH)

    arrays = ((x_ref, ax), (og_ref, aog))

    def copy(a, i):
        src, dst = arrays[a]
        own, other = xh, 1 - xh
        n = a * PER_ARRAY + i

        def same(where, target):
            return remote(n, where, where, target)

        if i in (UP, DOWN, ACROSS, SIB):
            return remote(n, src.at[0], piece(dst, own, y),
                          {UP: up, DOWN: down, ACROSS: across, SIB: sib}[i])
        if i == U2:
            return same(piece(dst, own, y - 1, 0), up)
        if i == D2:
            return same(piece(dst, own, y + 1, 1), down)
        if i == S_LO:
            return same(piece(dst, own, y - 1), sib)
        if i == S_HI:
            return same(piece(dst, own, y + 1), sib)
        if i in (C_UP, C_DOWN, C_SIB):
            return same(piece(dst, other, y), {C_UP: up, C_DOWN: down, C_SIB: sib}[i])
        if i == AX1:
            if along_y:
                return same(piece(dst, other, y - 1, 0), up)
            return same(piece(dst, own, y + 2, 0), across)
        if i == AX2:
            if along_y:
                return same(piece(dst, other, y + 1, 1), down)
            return same(piece(dst, own, y + 2, 1), across)
        if i == S_F1:
            return same(piece(dst, own, y + 2, 0), sib)
        if i == S_F2:
            return same(piece(dst, own, y + 2, 1), sib)
        if i == S_OLO:
            return same(piece(dst, other, y - 1), sib)
        if i == S_OHI:
            return same(piece(dst, other, y + 1), sib)
        if i == S_OF1:
            return same(piece(dst, other, y + 2, 0), sib)
        return same(piece(dst, other, y + 2, 1), sib)

    def start(a, *which):
        for i in which:
            copy(a, i).start()

    def arrived(a, *which):
        for i in which:
            copy(a, i).wait_recv()

    def local(i, src, dst):
        return pltpu.make_async_copy(src, dst, loc_sem.at[i])

    def own_copy(a):
        return local(a, arrays[a][0].at[0], piece(arrays[a][1], xh, y))

    loads = [local(2, wq_ref, wq_v), local(3, wo_ref, wo_v),
             local(4, mq_ref, mq_v), local(5, mo_ref, mo_v)]
    send_wq = remote(WQ, wq_ref, pq_v, partner)
    if relayed:
        send_wo = remote(WO, wo_ref, wrel, ahead)
        send_mo = remote(MO, mo_v, mrel, ahead)
        pass_wo = remote(WO2, wrel, po_v, ahead)
        pass_mo = remote(MO2, mrel, ro_v, ahead)
    else:
        send_wo = remote(WO, wo_ref, po_v, partner)
        send_mo = remote(MO, mo_v, ro_v, partner)

    def send_mq(d):
        at = pl.ds(pl.multiple_of(d * block, block), block)
        return remote(MQ + d, mq_v.at[at], rq_v.at[at], partner)

    own_copy(0).start()
    loads[0].start()
    barrier = pltpu.get_barrier_semaphore()
    everyone = [up, down, sib, across, partner, source]
    if relayed:
        everyone += [ahead, behind]
    for target in everyone:
        pl.semaphore_signal(barrier, inc=1, device_id=target, device_id_type=MESH)
    pl.semaphore_wait(barrier, len(everyone))
    start(0, UP, DOWN, ACROSS, SIB)
    if not along_y:
        send_wq.start()
        send_wo.start()
    own_copy(1).start()
    for c in loads[1:]:
        c.start()
    loads[0].wait()

    def near(a):
        arrived(a, UP)
        start(a, U2, S_LO)
        arrived(a, DOWN)
        start(a, D2, S_HI)

    def row(a):
        arrived(a, ACROSS)
        start(a, C_UP, C_DOWN, C_SIB)

    def far(a):
        arrived(a, U2)
        start(a, *((S_F1,) if along_y else (AX1, S_F1)))
        arrived(a, D2)
        start(a, *((S_F2,) if along_y else (AX2, S_F2)))

    def other_near(a):
        arrived(a, C_UP)
        start(a, *((AX1, S_OLO) if along_y else (S_OLO,)))
        arrived(a, C_DOWN)
        start(a, *((AX2, S_OHI) if along_y else (S_OHI,)))

    def other_far(a):
        arrived(a, AX1)
        start(a, S_OF1)
        arrived(a, AX2)
        start(a, S_OF2)

    def second_array(late):
        if along_y and not late:
            start(1, ACROSS)
            send_wq.start()
            send_wo.start()
        if late == along_y:
            start(1, *((UP, DOWN, SIB) if along_y else (UP, DOWN, ACROSS, SIB)))

    def when(i, k, *steps):
        @pl.when(i == k)
        def _():
            for s in steps:
                s()

    def chunk_at(i):
        side = pick(i, (0, 0, 0, 1, 0, 1, 1, 1))
        move_y = pick(i, (0, 3, 1, 0, 2, 3, 1, 2))
        return lax.rem(xh + side, 2) * 4 + lax.rem(y + move_y, 4)

    def tables(m):
        hc, hs = hc_ref[pl.ds(m, 1), :], hs_ref[pl.ds(m, 1), :]
        lc, ls = lc_ref[...], ls_ref[...]
        return hc * lc - hs * ls, hs * lc + hc * ls

    def turned(t):
        return pltpu.roll(t, head_dim // 2, 1)

    def project(i, _):
        when(i, 0, lambda: own_copy(0).wait(), lambda: arrived(0, SIB))
        when(i, 1, lambda: near(0), lambda: row(0), lambda: arrived(0, S_LO))
        when(i, 2, lambda: arrived(0, S_HI))
        when(i, 3, lambda: far(0), lambda: second_array(False), lambda: arrived(0, C_SIB))
        when(i, 4, lambda: arrived(0, S_F1, S_F2))
        when(i, 5, lambda: other_near(0), lambda: second_array(True), lambda: arrived(0, S_OLO))
        when(i, 6, lambda: other_far(0), lambda: arrived(0, S_OHI))
        when(i, 7, lambda: arrived(0, S_OF1, S_OF2))
        m = chunk_at(i)

        columns = [slice(c, c + head_dim) for c in range(0, width, head_dim)]
        squares = jnp.zeros((block, head_dim), F32)
        for at in columns:
            t = ax[m, :, at].astype(F32)
            squares = squares + t * t
        stats = lax.rsqrt(jnp.sum(squares, -1, keepdims=True) * (1.0 / width) + EPSILON)
        for at in columns:
            n_s[m, :, at] = (ax[m, :, at].astype(F32) * stats * gain_ref[:, at]).astype(BF16)
        proj = jnp.dot(n_s[m], wq_v[...], preferred_element_type=F32) * in_scale
        cos, sin = tables(m)
        q = proj[:, :head_dim]
        k = proj[:, head_dim:2 * head_dim]
        q = (q * cos + turned(q) * sin).astype(BF16)
        k = (k * cos + turned(k) * sin).astype(BF16)
        v = proj[:, 2 * head_dim:].astype(BF16)
        q_s[m], k_s[m], v_s[m] = q, k, v
        qt_s[m], kt_s[m], vt_s[m] = q.T, k.T, v.T
        dk_s[m] = jnp.zeros_like(dk_s[m])
        dv_s[m] = jnp.zeros_like(dv_s[m])
        return 0

    lax.fori_loop(0, chunks, project, 0)

    row_pos = lax.broadcasted_iota(jnp.int32, (block, block), 0)
    col_pos = lax.broadcasted_iota(jnp.int32, (block, block), 1)

    def folded(t, op):
        return op(t.reshape(block // 8, 8, block), axis=0)

    def forward(m, _):
        if relayed:
            when(m, 1, send_wo.wait_recv, pass_wo.start)
        when(m, 5, lambda: near(1), lambda: row(1))
        queries = qt_s[m]

        def scores(j, top):
            for u in (2 * j, 2 * j + 1):
                s = jnp.dot(k_s[u], queries, preferred_element_type=F32) * scale
                s = jnp.where(row_pos + u * block <= col_pos + m * block, s, -jnp.inf)
                s_s[u] = s
                top = jnp.maximum(top, folded(s, jnp.max))
            return top

        top = lax.fori_loop(0, (m + 2) // 2, scores, jnp.full((8, block), -jnp.inf, F32))
        top = jnp.max(top, 0, keepdims=True)

        def exps(j, total):
            for u in (2 * j, 2 * j + 1):
                e = jnp.exp(s_s[u] - top)
                s_s[u] = e
                total = total + folded(e, jnp.sum)
            return total

        total = lax.fori_loop(0, (m + 2) // 2, exps, jnp.zeros((8, block), F32))
        inverse = 1.0 / jnp.sum(total, 0, keepdims=True)

        def values(j, out):
            for u in (2 * j, 2 * j + 1):
                p = (s_s[u] * inverse).astype(BF16)
                p_s[m, u] = p
                out = out + jnp.dot(vt_s[u], p, preferred_element_type=F32)
            return out

        out = lax.fori_loop(0, (m + 2) // 2, values, jnp.zeros((head_dim, block), F32))
        o_s[m] = out
        att_t[m] = out.astype(BF16)
        return 0

    lax.fori_loop(0, chunks, forward, 0)
    for c in loads[1:]:
        c.wait()
    go_s[...] = jnp.zeros_like(go_s)

    def backward(i, _):
        when(i, 0, lambda: own_copy(1).wait(), lambda: arrived(1, SIB))
        when(i, 1, lambda: far(1), lambda: arrived(1, S_LO))
        when(i, 2, lambda: arrived(1, S_HI))
        when(i, 3, lambda: arrived(1, C_SIB))
        when(i, 4, lambda: arrived(1, S_F1, S_F2), lambda: other_near(1))
        when(i, 5, lambda: arrived(1, S_OLO))
        when(i, 6, lambda: arrived(1, S_OHI))
        when(i, 7, lambda: other_far(1), lambda: arrived(1, S_OF1, S_OF2))
        m = chunk_at(i)
        da = (dot_nt(aog[m], wo_v[...]) * out_scale).astype(BF16)
        da_t = da.T
        go_s[...] += jnp.dot(att_t[m], aog[m], preferred_element_type=F32)

        @pl.when(i == chunks - 1)
        def _():
            def moved(r, _):
                at = pl.ds(pl.multiple_of(r * 16, 16), 16)
                grad = (go_s[at, :] * out_scale).astype(BF16)
                mo_v[at, :] = (BETA * mo_v[at, :].astype(F32) + grad.astype(F32)).astype(BF16)
                return 0

            lax.fori_loop(0, head_dim // 16, moved, 0)
            send_mo.start()

        centre = jnp.sum(da_t.astype(F32) * o_s[m], 0, keepdims=True)
        q = q_s[m]

        def pair(j, dq):
            for u in (2 * j, 2 * j + 1):
                p = p_s[m, u]
                dp = jnp.dot(v_s[u], da_t, preferred_element_type=F32)
                ds = (p.astype(F32) * (dp - centre) * scale).astype(BF16)
                dk_s[u] += jnp.dot(ds, q, preferred_element_type=F32)
                dv_s[u] += jnp.dot(p, da, preferred_element_type=F32)
                dq = dq + jnp.dot(kt_s[u], ds, preferred_element_type=F32)
            return dq

        dq = lax.fori_loop(0, (m + 2) // 2, pair, jnp.zeros((head_dim, block), F32)).T
        cos, sin = tables(m)
        gp_s[m, :, :head_dim] = ((dq * cos - turned(dq) * sin) * in_scale).astype(BF16)
        return 0

    lax.fori_loop(0, chunks, backward, 0)

    def finish(m, _):
        cos, sin = tables(m)
        dk = dk_s[m]
        gp_s[m, :, head_dim:2 * head_dim] = (
            (dk * cos - turned(dk) * sin) * in_scale).astype(BF16)
        gp_s[m, :, 2 * head_dim:] = (dv_s[m] * in_scale).astype(BF16)
        return 0

    lax.fori_loop(0, chunks, finish, 0)

    def grads(d, _):
        at = pl.ds(pl.multiple_of(d * block, block), block)
        total = dot_tn(n_s[0, :, at], gp_s[0])
        for m in range(1, chunks):
            total = total + dot_tn(n_s[m, :, at], gp_s[m])
        mq_v[at, :] = (BETA * mq_v[at, :].astype(F32)
                       + total.astype(BF16).astype(F32)).astype(BF16)
        send_mq(d).start()
        return 0

    lax.fori_loop(0, width // block, grads, 0)
    rate = rate_ref[0]
    send_wq.wait()
    if relayed:
        send_wo.wait_send()
        pass_wo.wait()
        send_mo.wait()
        pass_mo.start()
    else:
        send_wo.wait()
        send_mo.wait()

    def outs_o(r, _):
        at = pl.ds(pl.multiple_of(r * 16, 16), 16)
        mine, theirs = mo_v[at, :], ro_v[at, :]
        nmo_ref[at, :] = average(mine, theirs)
        nwo_ref[at, :] = average(move(wo_v[at, :], mine, rate), move(po_v[at, :], theirs, rate))
        return 0

    if not relayed:
        lax.fori_loop(0, head_dim // 16, outs_o, 0)

    def outs_q(d, _):
        send_mq(d).wait()
        at = pl.ds(pl.multiple_of(d * block, block), block)
        mine, theirs = mq_v[at, :], rq_v[at, :]
        nmq_ref[at, :] = average(mine, theirs)
        nwq_ref[at, :] = average(move(wq_v[at, :], mine, rate), move(pq_v[at, :], theirs, rate))
        return 0

    lax.fori_loop(0, width // block, outs_q, 0)
    if relayed:
        pass_mo.wait()
        lax.fori_loop(0, head_dim // 16, outs_o, 0)

    for a in range(2):
        for i in range(PER_ARRAY):
            copy(a, i).wait_send()


def update(by, cid, rate, gain, tables, x, og, wq, wo, mq, mo):
    devices = lax.axis_size("fsdp")
    rows, width = x.shape[1:]
    block = 2 * rows
    chunks = devices // 2
    wide, head_dim = wq.shape[1], wo.shape[0]
    hbm = pl.BlockSpec(memory_space=pl.ANY)
    vmem = pl.BlockSpec(memory_space=pltpu.VMEM)
    n_copies = MQ + width // block

    def v(*shape, dtype=BF16):
        return pltpu.VMEM(shape, dtype)

    return pl.pallas_call(
        partial(kernel, by),
        out_shape=(
            jax.ShapeDtypeStruct(wq.shape, BF16), jax.ShapeDtypeStruct(wo.shape, BF16),
            jax.ShapeDtypeStruct(wq.shape, BF16), jax.ShapeDtypeStruct(wo.shape, BF16),
        ),
        in_specs=[pl.BlockSpec(memory_space=pltpu.SMEM)] + [vmem] * 5 + [hbm] * 6,
        out_specs=[vmem] * 4,
        scratch_shapes=[
            v(chunks, block, width), v(chunks, block, width), v(chunks, block, width),
            v(head_dim, width), v(head_dim, width),
            v(width, wide), v(head_dim, width), v(width, wide), v(head_dim, width),
            v(width, wide), v(head_dim, width), v(width, wide), v(head_dim, width),
            v(chunks, block, head_dim), v(chunks, block, head_dim), v(chunks, block, head_dim),
            v(chunks, head_dim, block), v(chunks, head_dim, block), v(chunks, head_dim, block),
            v(chunks, head_dim, block), v(chunks, head_dim, block, dtype=F32),
            v(chunks, block, block, dtype=F32), v(chunks, chunks, block, block),
            v(head_dim, width, dtype=F32),
            v(chunks, block, head_dim, dtype=F32), v(chunks, block, head_dim, dtype=F32),
            v(chunks, block, wide),
            pltpu.SemaphoreType.DMA((n_copies,)), pltpu.SemaphoreType.DMA((n_copies,)),
            pltpu.SemaphoreType.DMA((6,)),
        ],
        name=f"update_{by}",
        compiler_params=pltpu.CompilerParams(
            collective_id=cid, has_side_effects=True, vmem_limit_bytes=66_000_000),
    )(rate, gain, *tables, x, og, wq, wo, mq, mo)


def per_device(inputs, out_grad, norm_gain, w_qkv, w_out, mom_qkv, mom_out, step_index):
    rate = RATE * (step_index.astype(F32) + 1.0) / (4.0 * LEVELS)
    exponent = jnp.remainder(step_index[0], LEVELS)
    head_dim = w_out.shape[2]
    rows = inputs.shape[1]
    block, chunks = 2 * rows, lax.axis_size("fsdp") // 2
    half_width = head_dim // 2
    frequency = jnp.exp(
        -math.log(10000.0) * 2.0 * jnp.arange(half_width, dtype=F32) / head_dim)
    frequency = jnp.concatenate([frequency, frequency])
    high = (jnp.arange(chunks) * block).astype(F32)[:, None] * frequency[None, :]
    low = jnp.arange(block).astype(F32)[:, None] * frequency[None, :]
    sign = jnp.where(jnp.arange(head_dim) < half_width, -1.0, 1.0).astype(F32)
    tables = (jnp.cos(high), jnp.sin(high) * sign, jnp.cos(low), jnp.sin(low) * sign)
    outs = lax.switch(
        exponent, [partial(update, 1 << k, k) for k in range(LEVELS)],
        rate, norm_gain, tables, inputs, out_grad,
        w_qkv[0, 0], w_out[0, 0], mom_qkv[0, 0], mom_out[0, 0])
    return tuple(o[None, None] for o in outs)


def solution(mesh):
    return jax.shard_map(
        per_device,
        mesh=mesh,
        in_specs=(
            P("gossip", "fsdp", None),
            P("gossip", "fsdp", None),
            P("gossip", None),
            P("gossip", "fsdp", None, None),
            P("gossip", "fsdp", None, None),
            P("gossip", "fsdp", None, None),
            P("gossip", "fsdp", None, None),
            P(),
        ),
        out_specs=(
            P("gossip", "fsdp", None, None),
            P("gossip", "fsdp", None, None),
            P("gossip", "fsdp", None, None),
            P("gossip", "fsdp", None, None),
        ),
        check_vma=False,
    )
```

```python
from functools import partial
import math

import jax
import jax.numpy as jnp
from jax import lax
from jax.experimental import pallas as pl
from jax.experimental.pallas import tpu as pltpu
from jax.sharding import PartitionSpec as P

LEVELS = 3
BETA = 0.9
RATE = 0.1
EPSILON = 1e-05
FINE = 16
MESH = pl.DeviceIdType.MESH
F32 = jnp.float32
BF16 = jnp.bfloat16

(UP, UP_B, DOWN, DOWN_B, ACROSS, SIB, U2, D2, S_LO, S_HI, C_UP, C_DOWN, C_SIB, AX1, AX2, S_F1, S_F2,
 S_OLO, S_OHI, S_OF1, S_OF2) = range(21)
PER_ARRAY = 21
WQ = 2 * PER_ARRAY
WO = WQ + 1
MO = WQ + 2
WO2 = WQ + 3
MO2 = WQ + 4
MQ = WQ + 5


def dot_nt(a, b):
    return lax.dot_general(a, b, (((1,), (1,)), ((), ())), preferred_element_type=F32)


def dot_tn(a, b):
    return lax.dot_general(a, b, (((0,), (0,)), ((), ())), preferred_element_type=F32)


def pick(i, values):
    out = jnp.int32(values[0])
    for k in range(1, len(values)):
        out = jnp.where(i == k, jnp.int32(values[k]), out)
    return out


def average(own, other):
    return ((own.astype(F32) + other.astype(F32)) * 0.5).astype(BF16)


def move(weight, moved_m, rate):
    return (weight.astype(F32) - rate * moved_m.astype(F32)).astype(BF16)


def kernel(by, rate_ref, gain_ref, tab_ref,
           x_ref, og_ref, wq_ref, wo_ref, mq_ref, mo_ref,
           nwq_ref, nwo_ref, nmq_ref, nmo_ref,
           ax, aog, n_s, wrel, mrel, wq_v, wo_v, mq_v, mo_v, pq_v, po_v, rq_v, ro_v,
           lc_s, ls_s, q_s, k_s, v_s, qt_s, kt_s, vt_s, att_t, o_s, s_s, p_s, go_s, dk_s, dv_s, gp_s,
           send_sem, recv_sem, loc_sem):
    g = lax.axis_index("gossip")
    f = lax.axis_index("fsdp")
    n_g = lax.axis_size("gossip")
    core = lax.rem(f, 2)
    y = lax.rem(f // 2, 4)
    xh = f // 8
    chunks, block, width = ax.shape
    rows = block // 2
    half = rows // 2
    head_dim = wo_v.shape[0]
    out_scale = 1.0 / math.sqrt(lax.axis_size("fsdp") * head_dim)
    in_scale = 1.0 / math.sqrt(width)
    scale = 1.0 / math.sqrt(head_dim)

    def dev(xx, yy, cc):
        return xx * 8 + lax.rem(yy + 4, 4) * 2 + cc

    up = (g, dev(xh, y + 1, core))
    down = (g, dev(xh, y - 1, core))
    sib = (g, dev(xh, y, 1 - core))
    across = (g, dev(1 - xh, y, core))
    partner = (lax.rem(g + by, n_g), f)
    source = (lax.rem(g - by + n_g, n_g), f)
    leg = 6
    relayed = n_g - by == 2 * leg
    ahead = (lax.rem(g - leg + n_g, n_g), f)
    behind = (lax.rem(g + leg, n_g), f)
    along_y = by == 1

    def chunk(side, yy):
        return side * 4 + lax.rem(yy + 4, 4)

    def piece(dst, side, yy, part=None):
        first = pl.multiple_of(core * rows, rows)
        if part is None:
            return dst.at[chunk(side, yy), pl.ds(first, rows)]
        return dst.at[chunk(side, yy), pl.ds(pl.multiple_of(first + part * half, half), half)]

    def remote(i, src, dst, target):
        return pltpu.make_async_remote_copy(
            src_ref=src, dst_ref=dst, send_sem=send_sem.at[i], recv_sem=recv_sem.at[i],
            device_id=target, device_id_type=MESH)

    arrays = ((x_ref, ax), (og_ref, aog))

    def copy(a, i):
        src, dst = arrays[a]
        own, other = xh, 1 - xh
        n = a * PER_ARRAY + i

        def same(where, target):
            return remote(n, where, where, target)

        if i in (ACROSS, SIB):
            return remote(n, src.at[0], piece(dst, own, y), {ACROSS: across, SIB: sib}[i])
        if i in (UP, UP_B, DOWN, DOWN_B):
            part = 0 if i in (UP, DOWN_B) else 1
            return remote(n, src.at[0, pl.ds(part * half, half)], piece(dst, own, y, part),
                          up if i in (UP, UP_B) else down)
        if i == U2:
            return same(piece(dst, own, y - 1, 0), up)
        if i == D2:
            return same(piece(dst, own, y + 1, 1), down)
        if i == S_LO:
            return same(piece(dst, own, y - 1), sib)
        if i == S_HI:
            return same(piece(dst, own, y + 1), sib)
        if i in (C_UP, C_DOWN, C_SIB):
            return same(piece(dst, other, y), {C_UP: up, C_DOWN: down, C_SIB: sib}[i])
        if i == AX1:
            if along_y:
                return same(piece(dst, other, y - 1, 0), up)
            return same(piece(dst, own, y + 2, 0), across)
        if i == AX2:
            if along_y:
                return same(piece(dst, other, y + 1, 1), down)
            return same(piece(dst, own, y + 2, 1), across)
        if i == S_F1:
            return same(piece(dst, own, y + 2, 0), sib)
        if i == S_F2:
            return same(piece(dst, own, y + 2, 1), sib)
        if i == S_OLO:
            return same(piece(dst, other, y - 1), sib)
        if i == S_OHI:
            return same(piece(dst, other, y + 1), sib)
        if i == S_OF1:
            return same(piece(dst, other, y + 2, 0), sib)
        return same(piece(dst, other, y + 2, 1), sib)

    def start(a, *which):
        for i in which:
            copy(a, i).start()

    def arrived(a, *which):
        for i in which:
            copy(a, i).wait_recv()

    def local(i, src, dst):
        return pltpu.make_async_copy(src, dst, loc_sem.at[i])

    def own_copy(a):
        return local(a, arrays[a][0].at[0], piece(arrays[a][1], xh, y))

    loads = [local(2, wq_ref, wq_v), local(3, wo_ref, wo_v),
             local(4, mq_ref, mq_v), local(5, mo_ref, mo_v)]
    send_wq = remote(WQ, wq_ref, pq_v, partner)
    if relayed:
        send_wo = remote(WO, wo_ref, wrel, ahead)
        send_mo = remote(MO, mo_v, mrel, ahead)
        pass_wo = remote(WO2, wrel, po_v, ahead)
        pass_mo = remote(MO2, mrel, ro_v, ahead)
    else:
        send_wo = remote(WO, wo_ref, po_v, partner)
        send_mo = remote(MO, mo_v, ro_v, partner)

    def send_mq(d):
        at = pl.ds(pl.multiple_of(d * block, block), block)
        return remote(MQ + d, mq_v.at[at], rq_v.at[at], partner)

    own_copy(0).start()
    loads[0].start()
    barrier = pltpu.get_barrier_semaphore()
    everyone = [up, down, sib, across, partner, source]
    if relayed:
        everyone += [ahead, behind]
    for target in everyone:
        pl.semaphore_signal(barrier, inc=1, device_id=target, device_id_type=MESH)
    pl.semaphore_wait(barrier, len(everyone))
    start(0, UP, DOWN, UP_B, DOWN_B, ACROSS, SIB)
    if not along_y:
        send_wq.start()
        send_wo.start()
    own_copy(1).start()
    for c in loads[1:]:
        c.start()
    loads[0].wait()
    step = block // FINE
    fc, fs = tab_ref[0, pl.ds(chunks + FINE, step), :], tab_ref[1, pl.ds(chunks + FINE, step), :]
    for c in range(FINE):
        at = pl.ds(c * step, step)
        cc, cs = tab_ref[0, pl.ds(chunks + c, 1), :], tab_ref[1, pl.ds(chunks + c, 1), :]
        lc_s[at, :] = cc * fc - cs * fs
        ls_s[at, :] = cs * fc + cc * fs

    def near(a):
        arrived(a, UP)
        start(a, U2)
        arrived(a, DOWN)
        start(a, D2)

    def near_rest(a):
        arrived(a, UP_B)
        start(a, S_LO)
        arrived(a, DOWN_B)
        start(a, S_HI)

    def row(a):
        arrived(a, ACROSS)
        start(a, C_UP, C_DOWN, C_SIB)

    def far(a):
        arrived(a, U2)
        start(a, *((S_F1,) if along_y else (AX1, S_F1)))
        arrived(a, D2)
        start(a, *((S_F2,) if along_y else (AX2, S_F2)))

    def other_near(a):
        arrived(a, C_UP)
        start(a, *((AX1, S_OLO) if along_y else (S_OLO,)))
        arrived(a, C_DOWN)
        start(a, *((AX2, S_OHI) if along_y else (S_OHI,)))

    def other_far(a):
        arrived(a, AX1)
        start(a, S_OF1)
        arrived(a, AX2)
        start(a, S_OF2)

    def second_array(late):
        if along_y and not late:
            start(1, ACROSS)
            send_wq.start()
            send_wo.start()
        if late == along_y:
            start(1, UP, DOWN, UP_B, DOWN_B, *((SIB,) if along_y else (ACROSS, SIB)))

    def when(i, k, *steps):
        @pl.when(i == k)
        def _():
            for s in steps:
                s()

    def chunk_at(i):
        side = pick(i, (0, 0, 0, 1, 0, 1, 1, 1))
        move_y = pick(i, (0, 3, 1, 0, 2, 3, 1, 2))
        return lax.rem(xh + side, 2) * 4 + lax.rem(y + move_y, 4)

    def tables(m):
        hc, hs = tab_ref[0, pl.ds(m, 1), :], tab_ref[1, pl.ds(m, 1), :]
        lc, ls = lc_s[...], ls_s[...]
        return hc * lc - hs * ls, hs * lc + hc * ls

    def turned(t):
        return pltpu.roll(t, head_dim // 2, 1)

    def project(i, _):
        when(i, 0, lambda: own_copy(0).wait(), lambda: arrived(0, SIB),
             lambda: near(0))
        when(i, 1, lambda: near_rest(0), lambda: row(0), lambda: arrived(0, S_LO))
        when(i, 2, lambda: arrived(0, S_HI))
        when(i, 3, lambda: far(0), lambda: second_array(False), lambda: arrived(0, C_SIB))
        when(i, 4, lambda: arrived(0, S_F1, S_F2))
        when(i, 5, lambda: other_near(0), lambda: second_array(True), lambda: arrived(0, S_OLO))
        when(i, 7 if along_y else 6, lambda: other_far(0))
        when(i, 6, lambda: arrived(0, S_OHI))
        when(i, 7, lambda: arrived(0, S_OF1, S_OF2))
        m = chunk_at(i)

        columns = [slice(c, c + head_dim) for c in range(0, width, head_dim)]
        squares = jnp.zeros((block, head_dim), F32)
        for at in columns:
            t = ax[m, :, at].astype(F32)
            squares = squares + t * t
        stats = lax.rsqrt(jnp.sum(squares, -1, keepdims=True) * (1.0 / width) + EPSILON)
        for at in columns:
            n_s[m, :, at] = (ax[m, :, at].astype(F32) * stats * gain_ref[:, at]).astype(BF16)
        proj = jnp.dot(n_s[m], wq_v[...], preferred_element_type=F32) * in_scale
        cos, sin = tables(m)
        q = proj[:, :head_dim]
        k = proj[:, head_dim:2 * head_dim]
        q = (q * cos + turned(q) * sin).astype(BF16)
        k = (k * cos + turned(k) * sin).astype(BF16)
        v = proj[:, 2 * head_dim:].astype(BF16)
        q_s[m], k_s[m], v_s[m] = q, k, v
        qt_s[m], kt_s[m], vt_s[m] = q.T, k.T, v.T
        dk_s[m] = jnp.zeros_like(dk_s[m])
        dv_s[m] = jnp.zeros_like(dv_s[m])
        return 0

    lax.fori_loop(0, chunks, project, 0)

    row_pos = lax.broadcasted_iota(jnp.int32, (block, block), 0)
    col_pos = lax.broadcasted_iota(jnp.int32, (block, block), 1)

    def folded(t, op):
        return op(t.reshape(block // 8, 8, block), axis=0)

    def forward(m, _):
        if relayed:
            when(m, 1, send_wo.wait_recv, pass_wo.start)
        when(m, 4 if along_y else 0, lambda: near(1))
        when(m, 7 if along_y else 5, lambda: near_rest(1), lambda: row(1))
        if not along_y:
            when(m, 7, lambda: far(1))
        queries = qt_s[m]

        def scores(j, top):
            for u in (2 * j, 2 * j + 1):
                s = jnp.dot(k_s[u], queries, preferred_element_type=F32) * scale
                s = jnp.where(row_pos + u * block <= col_pos + m * block, s, -jnp.inf)
                s_s[u] = s
                top = jnp.maximum(top, folded(s, jnp.max))
            return top

        top = lax.fori_loop(0, (m + 2) // 2, scores, jnp.full((8, block), -jnp.inf, F32))
        top = jnp.max(top, 0, keepdims=True)

        def exps(j, total):
            for u in (2 * j, 2 * j + 1):
                e = jnp.exp(s_s[u] - top)
                s_s[u] = e
                total = total + folded(e, jnp.sum)
            return total

        total = lax.fori_loop(0, (m + 2) // 2, exps, jnp.zeros((8, block), F32))
        inverse = 1.0 / jnp.sum(total, 0, keepdims=True)

        def values(j, out):
            for u in (2 * j, 2 * j + 1):
                p = (s_s[u] * inverse).astype(BF16)
                p_s[m, u] = p
                out = out + jnp.dot(vt_s[u], p, preferred_element_type=F32)
            return out

        out = lax.fori_loop(0, (m + 2) // 2, values, jnp.zeros((head_dim, block), F32))
        o_s[m] = out
        att_t[m] = out.astype(BF16)
        return 0

    lax.fori_loop(0, chunks, forward, 0)
    for c in loads[1:]:
        c.wait()
    go_s[...] = jnp.zeros_like(go_s)

    def backward(i, _):
        when(i, 0, lambda: own_copy(1).wait(), lambda: arrived(1, SIB))
        when(i, 1, lambda: arrived(1, S_LO))
        when(i, 2, lambda: arrived(1, S_HI))
        if along_y:
            when(i, 3, lambda: far(1))
        when(i, 3, lambda: arrived(1, C_SIB))
        when(i, 4, lambda: arrived(1, S_F1, S_F2))
        when(i, 5, lambda: other_near(1), lambda: arrived(1, S_OLO))
        when(i, 7 if along_y else 6, lambda: other_far(1))
        when(i, 6, lambda: arrived(1, S_OHI))
        when(i, 7, lambda: arrived(1, S_OF1, S_OF2))
        m = chunk_at(i)
        da = (dot_nt(aog[m], wo_v[...]) * out_scale).astype(BF16)
        da_t = da.T
        go_s[...] += jnp.dot(att_t[m], aog[m], preferred_element_type=F32)

        @pl.when(i == chunks - 1)
        def _():
            def moved(r, _):
                at = pl.ds(pl.multiple_of(r * 16, 16), 16)
                grad = (go_s[at, :] * out_scale).astype(BF16)
                mo_v[at, :] = (BETA * mo_v[at, :].astype(F32) + grad.astype(F32)).astype(BF16)
                return 0

            lax.fori_loop(0, head_dim // 16, moved, 0)
            send_mo.start()

        centre = jnp.sum(da_t.astype(F32) * o_s[m], 0, keepdims=True)
        q = q_s[m]

        def pair(j, dq):
            for u in (2 * j, 2 * j + 1):
                p = p_s[m, u]
                dp = jnp.dot(v_s[u], da_t, preferred_element_type=F32)
                ds = (p.astype(F32) * (dp - centre) * scale).astype(BF16)
                dk_s[u] += jnp.dot(ds, q, preferred_element_type=F32)
                dv_s[u] += jnp.dot(p, da, preferred_element_type=F32)
                dq = dq + jnp.dot(kt_s[u], ds, preferred_element_type=F32)
            return dq

        dq = lax.fori_loop(0, (m + 2) // 2, pair, jnp.zeros((head_dim, block), F32)).T
        cos, sin = tables(m)
        gp_s[m, :, :head_dim] = ((dq * cos - turned(dq) * sin) * in_scale).astype(BF16)
        return 0

    lax.fori_loop(0, chunks, backward, 0)

    def finish(m, _):
        cos, sin = tables(m)
        dk = dk_s[m]
        gp_s[m, :, head_dim:2 * head_dim] = (
            (dk * cos - turned(dk) * sin) * in_scale).astype(BF16)
        gp_s[m, :, 2 * head_dim:] = (dv_s[m] * in_scale).astype(BF16)
        return 0

    lax.fori_loop(0, chunks, finish, 0)

    def grads(d, _):
        at = pl.ds(pl.multiple_of(d * block, block), block)
        total = dot_tn(n_s[0, :, at], gp_s[0])
        for m in range(1, chunks):
            total = total + dot_tn(n_s[m, :, at], gp_s[m])
        mq_v[at, :] = (BETA * mq_v[at, :].astype(F32)
                       + total.astype(BF16).astype(F32)).astype(BF16)
        send_mq(d).start()
        return 0

    lax.fori_loop(0, width // block, grads, 0)
    rate = rate_ref[0]
    send_wq.wait()
    if relayed:
        send_wo.wait_send()
        pass_wo.wait()
        send_mo.wait()
        pass_mo.start()
    else:
        send_wo.wait()
        send_mo.wait()

    def outs_o(r, _):
        at = pl.ds(pl.multiple_of(r * 16, 16), 16)
        mine, theirs = mo_v[at, :], ro_v[at, :]
        nmo_ref[at, :] = average(mine, theirs)
        nwo_ref[at, :] = average(move(wo_v[at, :], mine, rate), move(po_v[at, :], theirs, rate))
        return 0

    if not relayed:
        lax.fori_loop(0, head_dim // 16, outs_o, 0)

    def outs_q(d, _):
        send_mq(d).wait()
        at = pl.ds(pl.multiple_of(d * block, block), block)
        mine, theirs = mq_v[at, :], rq_v[at, :]
        nmq_ref[at, :] = average(mine, theirs)
        nwq_ref[at, :] = average(move(wq_v[at, :], mine, rate), move(pq_v[at, :], theirs, rate))
        return 0

    lax.fori_loop(0, width // block, outs_q, 0)
    if relayed:
        pass_mo.wait()
        lax.fori_loop(0, head_dim // 16, outs_o, 0)

    for a in range(2):
        for i in range(PER_ARRAY):
            copy(a, i).wait_send()


def update(by, cid, rate, gain, tables, x, og, wq, wo, mq, mo):
    devices = lax.axis_size("fsdp")
    rows, width = x.shape[1:]
    block = 2 * rows
    chunks = devices // 2
    wide, head_dim = wq.shape[1], wo.shape[0]
    hbm = pl.BlockSpec(memory_space=pl.ANY)
    vmem = pl.BlockSpec(memory_space=pltpu.VMEM)
    n_copies = MQ + width // block

    def v(*shape, dtype=BF16):
        return pltpu.VMEM(shape, dtype)

    return pl.pallas_call(
        partial(kernel, by),
        out_shape=(
            jax.ShapeDtypeStruct(wq.shape, BF16), jax.ShapeDtypeStruct(wo.shape, BF16),
            jax.ShapeDtypeStruct(wq.shape, BF16), jax.ShapeDtypeStruct(wo.shape, BF16),
        ),
        in_specs=[pl.BlockSpec(memory_space=pltpu.SMEM)] + [vmem] * 2 + [hbm] * 6,
        out_specs=[vmem] * 4,
        scratch_shapes=[
            v(chunks, block, width), v(chunks, block, width), v(chunks, block, width),
            v(head_dim, width), v(head_dim, width),
            v(width, wide), v(head_dim, width), v(width, wide), v(head_dim, width),
            v(width, wide), v(head_dim, width), v(width, wide), v(head_dim, width),
            v(block, head_dim, dtype=F32), v(block, head_dim, dtype=F32),
            v(chunks, block, head_dim), v(chunks, block, head_dim), v(chunks, block, head_dim),
            v(chunks, head_dim, block), v(chunks, head_dim, block), v(chunks, head_dim, block),
            v(chunks, head_dim, block), v(chunks, head_dim, block, dtype=F32),
            v(chunks, block, block, dtype=F32), v(chunks, chunks, block, block),
            v(head_dim, width, dtype=F32),
            v(chunks, block, head_dim, dtype=F32), v(chunks, block, head_dim, dtype=F32),
            v(chunks, block, wide),
            pltpu.SemaphoreType.DMA((n_copies,)), pltpu.SemaphoreType.DMA((n_copies,)),
            pltpu.SemaphoreType.DMA((6,)),
        ],
        name=f"update_{by}",
        compiler_params=pltpu.CompilerParams(
            collective_id=cid, has_side_effects=True, vmem_limit_bytes=66_000_000),
    )(rate, gain, tables, x, og, wq, wo, mq, mo)


def per_device(inputs, out_grad, norm_gain, w_qkv, w_out, mom_qkv, mom_out, step_index):
    rate = RATE * (step_index.astype(F32) + 1.0) / (4.0 * LEVELS)
    exponent = jnp.remainder(step_index[0], LEVELS)
    head_dim = w_out.shape[2]
    rows = inputs.shape[1]
    block, chunks = 2 * rows, lax.axis_size("fsdp") // 2
    half_width = head_dim // 2
    frequency = jnp.exp(
        -math.log(10000.0) * 2.0 * jnp.arange(half_width, dtype=F32) / head_dim)
    frequency = jnp.concatenate([frequency, frequency])
    step = block // FINE
    positions = jnp.concatenate(
        [jnp.arange(chunks) * block, jnp.arange(FINE) * step, jnp.arange(step)])
    angles = positions.astype(F32)[:, None] * frequency[None, :]
    sign = jnp.where(jnp.arange(head_dim) < half_width, -1.0, 1.0).astype(F32)
    tables = jnp.stack([jnp.cos(angles), jnp.sin(angles) * sign])
    outs = lax.switch(
        exponent, [partial(update, 1 << k, k) for k in range(LEVELS)],
        rate, norm_gain, tables, inputs, out_grad,
        w_qkv[0, 0], w_out[0, 0], mom_qkv[0, 0], mom_out[0, 0])
    return tuple(o[None, None] for o in outs)


def solution(mesh):
    return jax.shard_map(
        per_device,
        mesh=mesh,
        in_specs=(
            P("gossip", "fsdp", None),
            P("gossip", "fsdp", None),
            P("gossip", None),
            P("gossip", "fsdp", None, None),
            P("gossip", "fsdp", None, None),
            P("gossip", "fsdp", None, None),
            P("gossip", "fsdp", None, None),
            P(),
        ),
        out_specs=(
            P("gossip", "fsdp", None, None),
            P("gossip", "fsdp", None, None),
            P("gossip", "fsdp", None, None),
            P("gossip", "fsdp", None, None),
        ),
        check_vma=False,
    )
```

```python
from functools import partial
import math

import jax
import jax.numpy as jnp
from jax import lax
from jax.experimental import pallas as pl
from jax.experimental.pallas import tpu as pltpu
from jax.sharding import PartitionSpec as P

LEVELS = 3
BETA = 0.9
RATE = 0.1
EPSILON = 1e-05
FINE = 16
MESH = pl.DeviceIdType.MESH
F32 = jnp.float32
BF16 = jnp.bfloat16

(UP, UP_B, DOWN, DOWN_B, ACROSS, SIB, U2, D2, S_LO, S_HI, C_UP, C_DOWN, C_SIB, AX1, AX2, S_F1, S_F2,
 S_OLO, S_OHI, S_OF1, S_OF2) = range(21)
PER_ARRAY = 21
WQ = 2 * PER_ARRAY
WO = WQ + 1
MO = WQ + 2
WO2 = WQ + 3
MO2 = WQ + 4
MQ = WQ + 5


def dot_nt(a, b):
    return lax.dot_general(a, b, (((1,), (1,)), ((), ())), preferred_element_type=F32)


def dot_tn(a, b):
    return lax.dot_general(a, b, (((0,), (0,)), ((), ())), preferred_element_type=F32)


def pick(i, values):
    out = jnp.int32(values[0])
    for k in range(1, len(values)):
        out = jnp.where(i == k, jnp.int32(values[k]), out)
    return out


def average(own, other):
    return ((own.astype(F32) + other.astype(F32)) * 0.5).astype(BF16)


def move(weight, moved_m, rate):
    return (weight.astype(F32) - rate * moved_m.astype(F32)).astype(BF16)


def kernel(by, rate_ref, gain_ref, tab_ref,
           x_ref, og_ref, wq_ref, wo_ref, mq_ref, mo_ref,
           nwq_ref, nwo_ref, nmq_ref, nmo_ref,
           ax, aog, n_s, wrel, mrel, wq_v, wo_v, mq_v, mo_v, pq_v, po_v, rq_v, ro_v,
           lc_s, ls_s, q_s, k_s, v_s, qt_s, kt_s, vt_s, att_t, o_s, s_s, p_s, go_s, dk_s, dv_s, gp_s,
           send_sem, recv_sem, loc_sem):
    g = lax.axis_index("gossip")
    f = lax.axis_index("fsdp")
    n_g = lax.axis_size("gossip")
    core = lax.rem(f, 2)
    y = lax.rem(f // 2, 4)
    xh = f // 8
    chunks, block, width = ax.shape
    rows = block // 2
    half = rows // 2
    head_dim = wo_v.shape[0]
    out_scale = 1.0 / math.sqrt(lax.axis_size("fsdp") * head_dim)
    in_scale = 1.0 / math.sqrt(width)
    scale = 1.0 / math.sqrt(head_dim)

    def dev(xx, yy, cc):
        return xx * 8 + lax.rem(yy + 4, 4) * 2 + cc

    up = (g, dev(xh, y + 1, core))
    down = (g, dev(xh, y - 1, core))
    sib = (g, dev(xh, y, 1 - core))
    across = (g, dev(1 - xh, y, core))
    partner = (lax.rem(g + by, n_g), f)
    source = (lax.rem(g - by + n_g, n_g), f)
    leg = 6
    relayed = n_g - by == 2 * leg
    ahead = (lax.rem(g - leg + n_g, n_g), f)
    behind = (lax.rem(g + leg, n_g), f)
    along_y = by == 1

    def chunk(side, yy):
        return side * 4 + lax.rem(yy + 4, 4)

    def piece(dst, side, yy, part=None):
        first = pl.multiple_of(core * rows, rows)
        if part is None:
            return dst.at[chunk(side, yy), pl.ds(first, rows)]
        return dst.at[chunk(side, yy), pl.ds(pl.multiple_of(first + part * half, half), half)]

    def remote(i, src, dst, target):
        return pltpu.make_async_remote_copy(
            src_ref=src, dst_ref=dst, send_sem=send_sem.at[i], recv_sem=recv_sem.at[i],
            device_id=target, device_id_type=MESH)

    arrays = ((x_ref, ax), (og_ref, aog))

    def copy(a, i):
        src, dst = arrays[a]
        own, other = xh, 1 - xh
        n = a * PER_ARRAY + i

        def same(where, target):
            return remote(n, where, where, target)

        if i in (ACROSS, SIB):
            return remote(n, src.at[0], piece(dst, own, y), {ACROSS: across, SIB: sib}[i])
        if i in (UP, UP_B, DOWN, DOWN_B):
            part = 0 if i in (UP, DOWN_B) else 1
            return remote(n, src.at[0, pl.ds(part * half, half)], piece(dst, own, y, part),
                          up if i in (UP, UP_B) else down)
        if i == U2:
            return same(piece(dst, own, y - 1, 0), up)
        if i == D2:
            return same(piece(dst, own, y + 1, 1), down)
        if i == S_LO:
            return same(piece(dst, own, y - 1), sib)
        if i == S_HI:
            return same(piece(dst, own, y + 1), sib)
        if i in (C_UP, C_DOWN, C_SIB):
            return same(piece(dst, other, y), {C_UP: up, C_DOWN: down, C_SIB: sib}[i])
        if i == AX1:
            if along_y:
                return same(piece(dst, other, y - 1, 0), up)
            return same(piece(dst, own, y + 2, 0), across)
        if i == AX2:
            if along_y:
                return same(piece(dst, other, y + 1, 1), down)
            return same(piece(dst, own, y + 2, 1), across)
        if i == S_F1:
            return same(piece(dst, own, y + 2, 0), sib)
        if i == S_F2:
            return same(piece(dst, own, y + 2, 1), sib)
        if i == S_OLO:
            return same(piece(dst, other, y - 1), sib)
        if i == S_OHI:
            return same(piece(dst, other, y + 1), sib)
        if i == S_OF1:
            return same(piece(dst, other, y + 2, 0), sib)
        return same(piece(dst, other, y + 2, 1), sib)

    def start(a, *which):
        for i in which:
            copy(a, i).start()

    def arrived(a, *which):
        for i in which:
            copy(a, i).wait_recv()

    def local(i, src, dst):
        return pltpu.make_async_copy(src, dst, loc_sem.at[i])

    def own_copy(a):
        return local(a, arrays[a][0].at[0], piece(arrays[a][1], xh, y))

    loads = [local(2, wq_ref, wq_v), local(3, wo_ref, wo_v),
             local(4, mq_ref, mq_v), local(5, mo_ref, mo_v)]
    send_wq = remote(WQ, wq_ref, pq_v, partner)
    if relayed:
        send_wo = remote(WO, wo_ref, wrel, ahead)
        send_mo = remote(MO, mo_v, mrel, ahead)
        pass_wo = remote(WO2, wrel, po_v, ahead)
        pass_mo = remote(MO2, mrel, ro_v, ahead)
    else:
        send_wo = remote(WO, wo_ref, po_v, partner)
        send_mo = remote(MO, mo_v, ro_v, partner)

    def send_mq(d):
        at = pl.ds(pl.multiple_of(d * block, block), block)
        return remote(MQ + d, mq_v.at[at], rq_v.at[at], partner)

    own_copy(0).start()
    loads[0].start()
    barrier = pltpu.get_barrier_semaphore()
    everyone = [up, down, sib, across, partner, source]
    if relayed:
        everyone += [ahead, behind]
    for target in everyone:
        pl.semaphore_signal(barrier, inc=1, device_id=target, device_id_type=MESH)
    pl.semaphore_wait(barrier, len(everyone))
    start(0, UP, DOWN, UP_B, DOWN_B, ACROSS, SIB)
    if not along_y:
        send_wq.start()
        send_wo.start()
    own_copy(1).start()
    for c in loads[1:]:
        c.start()
    loads[0].wait()
    step = block // FINE
    fc, fs = tab_ref[0, pl.ds(chunks + FINE, step), :], tab_ref[1, pl.ds(chunks + FINE, step), :]
    for c in range(FINE):
        at = pl.ds(c * step, step)
        cc, cs = tab_ref[0, pl.ds(chunks + c, 1), :], tab_ref[1, pl.ds(chunks + c, 1), :]
        lc_s[at, :] = cc * fc - cs * fs
        ls_s[at, :] = cs * fc + cc * fs

    def near(a):
        arrived(a, UP)
        start(a, U2)
        arrived(a, DOWN)
        start(a, D2)

    def near_rest(a):
        arrived(a, UP_B)
        start(a, S_LO)
        arrived(a, DOWN_B)
        start(a, S_HI)

    def row(a):
        if a == 0 or not along_y:
            arrived(a, ACROSS)
        start(a, C_UP, C_DOWN, C_SIB)
        if a == 0 and along_y:
            start(1, ACROSS)

    def far(a):
        arrived(a, U2)
        start(a, *((S_F1,) if along_y else (AX1, S_F1)))
        arrived(a, D2)
        start(a, *((S_F2,) if along_y else (AX2, S_F2)))

    def other_near(a):
        arrived(a, C_UP)
        start(a, *((AX1, S_OLO) if along_y else (S_OLO,)))
        arrived(a, C_DOWN)
        start(a, *((AX2, S_OHI) if along_y else (S_OHI,)))

    def other_far(a):
        arrived(a, AX1)
        start(a, S_OF1)
        arrived(a, AX2)
        start(a, S_OF2)

    def second_array(late):
        if along_y and late:
            arrived(1, ACROSS)
            send_wq.start()
            send_wo.start()
        if late == along_y:
            start(1, UP, DOWN, UP_B, DOWN_B, *((SIB,) if along_y else (ACROSS, SIB)))

    def when(i, k, *steps):
        @pl.when(i == k)
        def _():
            for s in steps:
                s()

    def chunk_at(i):
        side = pick(i, (0, 0, 0, 1, 0, 1, 1, 1))
        move_y = pick(i, (0, 3, 1, 0, 2, 3, 1, 2))
        return lax.rem(xh + side, 2) * 4 + lax.rem(y + move_y, 4)

    def tables(m):
        hc, hs = tab_ref[0, pl.ds(m, 1), :], tab_ref[1, pl.ds(m, 1), :]
        lc, ls = lc_s[...], ls_s[...]
        return hc * lc - hs * ls, hs * lc + hc * ls

    def turned(t):
        return pltpu.roll(t, head_dim // 2, 1)

    def project(i, _):
        when(i, 0, lambda: own_copy(0).wait(), lambda: arrived(0, SIB),
             lambda: near(0))
        when(i, 1, lambda: near_rest(0), lambda: row(0), lambda: arrived(0, S_LO))
        when(i, 2, lambda: arrived(0, S_HI))
        when(i, 3, lambda: far(0), lambda: second_array(False), lambda: arrived(0, C_SIB))
        when(i, 4, lambda: arrived(0, S_F1, S_F2))
        when(i, 5, lambda: other_near(0), lambda: second_array(True), lambda: arrived(0, S_OLO))
        when(i, 7 if along_y else 6, lambda: other_far(0))
        when(i, 6, lambda: arrived(0, S_OHI))
        when(i, 7, lambda: arrived(0, S_OF1, S_OF2))
        m = chunk_at(i)

        columns = [slice(c, c + head_dim) for c in range(0, width, head_dim)]
        squares = jnp.zeros((block, head_dim), F32)
        for at in columns:
            t = ax[m, :, at].astype(F32)
            squares = squares + t * t
        stats = lax.rsqrt(jnp.sum(squares, -1, keepdims=True) * (1.0 / width) + EPSILON)
        for at in columns:
            n_s[m, :, at] = (ax[m, :, at].astype(F32) * stats * gain_ref[:, at]).astype(BF16)
        proj = jnp.dot(n_s[m], wq_v[...], preferred_element_type=F32) * in_scale
        cos, sin = tables(m)
        q = proj[:, :head_dim]
        k = proj[:, head_dim:2 * head_dim]
        q = (q * cos + turned(q) * sin).astype(BF16)
        k = (k * cos + turned(k) * sin).astype(BF16)
        v = proj[:, 2 * head_dim:].astype(BF16)
        q_s[m], k_s[m], v_s[m] = q, k, v
        qt_s[m], kt_s[m], vt_s[m] = q.T, k.T, v.T
        dk_s[m] = jnp.zeros_like(dk_s[m])
        dv_s[m] = jnp.zeros_like(dv_s[m])
        return 0

    lax.fori_loop(0, chunks, project, 0)

    row_pos = lax.broadcasted_iota(jnp.int32, (block, block), 0)
    col_pos = lax.broadcasted_iota(jnp.int32, (block, block), 1)

    def folded(t, op):
        return op(t.reshape(block // 8, 8, block), axis=0)

    def forward(m, _):
        if relayed:
            when(m, 1, send_wo.wait_recv, pass_wo.start)
        when(m, 4 if along_y else 0, lambda: near(1))
        when(m, 7 if along_y else 5, lambda: near_rest(1), lambda: row(1))
        if not along_y:
            when(m, 7, lambda: far(1))
        queries = qt_s[m]

        def scores(j, top):
            for u in (2 * j, 2 * j + 1):
                s = jnp.dot(k_s[u], queries, preferred_element_type=F32) * scale
                s = jnp.where(row_pos + u * block <= col_pos + m * block, s, -jnp.inf)
                s_s[u] = s
                top = jnp.maximum(top, folded(s, jnp.max))
            return top

        top = lax.fori_loop(0, (m + 2) // 2, scores, jnp.full((8, block), -jnp.inf, F32))
        top = jnp.max(top, 0, keepdims=True)

        def exps(j, total):
            for u in (2 * j, 2 * j + 1):
                e = jnp.exp(s_s[u] - top)
                s_s[u] = e
                total = total + folded(e, jnp.sum)
            return total

        total = lax.fori_loop(0, (m + 2) // 2, exps, jnp.zeros((8, block), F32))
        inverse = 1.0 / jnp.sum(total, 0, keepdims=True)

        def values(j, out):
            for u in (2 * j, 2 * j + 1):
                p = (s_s[u] * inverse).astype(BF16)
                p_s[m, u] = p
                out = out + jnp.dot(vt_s[u], p, preferred_element_type=F32)
            return out

        out = lax.fori_loop(0, (m + 2) // 2, values, jnp.zeros((head_dim, block), F32))
        o_s[m] = out
        att_t[m] = out.astype(BF16)
        return 0

    lax.fori_loop(0, chunks, forward, 0)
    for c in loads[1:]:
        c.wait()
    go_s[...] = jnp.zeros_like(go_s)

    def backward(i, _):
        when(i, 0, lambda: own_copy(1).wait(), lambda: arrived(1, SIB))
        when(i, 1, lambda: arrived(1, S_LO))
        when(i, 2, lambda: arrived(1, S_HI))
        if along_y:
            when(i, 3, lambda: far(1))
        when(i, 3, lambda: arrived(1, C_SIB))
        when(i, 4, lambda: arrived(1, S_F1, S_F2))
        when(i, 5, lambda: other_near(1), lambda: arrived(1, S_OLO))
        when(i, 7 if along_y else 6, lambda: other_far(1))
        when(i, 6, lambda: arrived(1, S_OHI))
        when(i, 7, lambda: arrived(1, S_OF1, S_OF2))
        m = chunk_at(i)
        da = (dot_nt(aog[m], wo_v[...]) * out_scale).astype(BF16)
        da_t = da.T
        go_s[...] += jnp.dot(att_t[m], aog[m], preferred_element_type=F32)

        @pl.when(i == chunks - 1)
        def _():
            def moved(r, _):
                at = pl.ds(pl.multiple_of(r * 16, 16), 16)
                grad = (go_s[at, :] * out_scale).astype(BF16)
                mo_v[at, :] = (BETA * mo_v[at, :].astype(F32) + grad.astype(F32)).astype(BF16)
                return 0

            lax.fori_loop(0, head_dim // 16, moved, 0)
            send_mo.start()

        centre = jnp.sum(da_t.astype(F32) * o_s[m], 0, keepdims=True)
        q = q_s[m]

        def pair(j, dq):
            for u in (2 * j, 2 * j + 1):
                p = p_s[m, u]
                dp = jnp.dot(v_s[u], da_t, preferred_element_type=F32)
                ds = (p.astype(F32) * (dp - centre) * scale).astype(BF16)
                dk_s[u] += jnp.dot(ds, q, preferred_element_type=F32)
                dv_s[u] += jnp.dot(p, da, preferred_element_type=F32)
                dq = dq + jnp.dot(kt_s[u], ds, preferred_element_type=F32)
            return dq

        dq = lax.fori_loop(0, (m + 2) // 2, pair, jnp.zeros((head_dim, block), F32)).T
        cos, sin = tables(m)
        gp_s[m, :, :head_dim] = ((dq * cos - turned(dq) * sin) * in_scale).astype(BF16)
        return 0

    lax.fori_loop(0, chunks, backward, 0)

    def finish(m, _):
        cos, sin = tables(m)
        dk = dk_s[m]
        gp_s[m, :, head_dim:2 * head_dim] = (
            (dk * cos - turned(dk) * sin) * in_scale).astype(BF16)
        gp_s[m, :, 2 * head_dim:] = (dv_s[m] * in_scale).astype(BF16)
        return 0

    lax.fori_loop(0, chunks, finish, 0)

    def grads(d, _):
        at = pl.ds(pl.multiple_of(d * block, block), block)
        total = dot_tn(n_s[0, :, at], gp_s[0])
        for m in range(1, chunks):
            total = total + dot_tn(n_s[m, :, at], gp_s[m])
        mq_v[at, :] = (BETA * mq_v[at, :].astype(F32)
                       + total.astype(BF16).astype(F32)).astype(BF16)
        send_mq(d).start()
        return 0

    lax.fori_loop(0, width // block, grads, 0)
    rate = rate_ref[0]
    send_wq.wait()
    if relayed:
        send_wo.wait_send()
        pass_wo.wait()
        send_mo.wait()
        pass_mo.start()
    else:
        send_wo.wait()
        send_mo.wait()

    def outs_o(r, _):
        at = pl.ds(pl.multiple_of(r * 16, 16), 16)
        mine, theirs = mo_v[at, :], ro_v[at, :]
        nmo_ref[at, :] = average(mine, theirs)
        nwo_ref[at, :] = average(move(wo_v[at, :], mine, rate), move(po_v[at, :], theirs, rate))
        return 0

    if not relayed:
        lax.fori_loop(0, head_dim // 16, outs_o, 0)

    def outs_q(d, _):
        send_mq(d).wait()
        at = pl.ds(pl.multiple_of(d * block, block), block)
        mine, theirs = mq_v[at, :], rq_v[at, :]
        nmq_ref[at, :] = average(mine, theirs)
        nwq_ref[at, :] = average(move(wq_v[at, :], mine, rate), move(pq_v[at, :], theirs, rate))
        return 0

    lax.fori_loop(0, width // block, outs_q, 0)
    if relayed:
        pass_mo.wait()
        lax.fori_loop(0, head_dim // 16, outs_o, 0)

    for a in range(2):
        for i in range(PER_ARRAY):
            copy(a, i).wait_send()


def update(by, cid, rate, gain, tables, x, og, wq, wo, mq, mo):
    devices = lax.axis_size("fsdp")
    rows, width = x.shape[1:]
    block = 2 * rows
    chunks = devices // 2
    wide, head_dim = wq.shape[1], wo.shape[0]
    hbm = pl.BlockSpec(memory_space=pl.ANY)
    vmem = pl.BlockSpec(memory_space=pltpu.VMEM)
    n_copies = MQ + width // block

    def v(*shape, dtype=BF16):
        return pltpu.VMEM(shape, dtype)

    return pl.pallas_call(
        partial(kernel, by),
        out_shape=(
            jax.ShapeDtypeStruct(wq.shape, BF16), jax.ShapeDtypeStruct(wo.shape, BF16),
            jax.ShapeDtypeStruct(wq.shape, BF16), jax.ShapeDtypeStruct(wo.shape, BF16),
        ),
        in_specs=[pl.BlockSpec(memory_space=pltpu.SMEM)] + [vmem] * 2 + [hbm] * 6,
        out_specs=[vmem] * 4,
        scratch_shapes=[
            v(chunks, block, width), v(chunks, block, width), v(chunks, block, width),
            v(head_dim, width), v(head_dim, width),
            v(width, wide), v(head_dim, width), v(width, wide), v(head_dim, width),
            v(width, wide), v(head_dim, width), v(width, wide), v(head_dim, width),
            v(block, head_dim, dtype=F32), v(block, head_dim, dtype=F32),
            v(chunks, block, head_dim), v(chunks, block, head_dim), v(chunks, block, head_dim),
            v(chunks, head_dim, block), v(chunks, head_dim, block), v(chunks, head_dim, block),
            v(chunks, head_dim, block), v(chunks, head_dim, block, dtype=F32),
            v(chunks, block, block, dtype=F32), v(chunks, chunks, block, block),
            v(head_dim, width, dtype=F32),
            v(chunks, block, head_dim, dtype=F32), v(chunks, block, head_dim, dtype=F32),
            v(chunks, block, wide),
            pltpu.SemaphoreType.DMA((n_copies,)), pltpu.SemaphoreType.DMA((n_copies,)),
            pltpu.SemaphoreType.DMA((6,)),
        ],
        name=f"update_{by}",
        compiler_params=pltpu.CompilerParams(
            collective_id=cid, has_side_effects=True, vmem_limit_bytes=66_000_000),
    )(rate, gain, tables, x, og, wq, wo, mq, mo)


def per_device(inputs, out_grad, norm_gain, w_qkv, w_out, mom_qkv, mom_out, step_index):
    rate = RATE * (step_index.astype(F32) + 1.0) / (4.0 * LEVELS)
    exponent = jnp.remainder(step_index[0], LEVELS)
    head_dim = w_out.shape[2]
    rows = inputs.shape[1]
    block, chunks = 2 * rows, lax.axis_size("fsdp") // 2
    half_width = head_dim // 2
    frequency = jnp.exp(
        -math.log(10000.0) * 2.0 * jnp.arange(half_width, dtype=F32) / head_dim)
    frequency = jnp.concatenate([frequency, frequency])
    step = block // FINE
    positions = jnp.concatenate(
        [jnp.arange(chunks) * block, jnp.arange(FINE) * step, jnp.arange(step)])
    angles = positions.astype(F32)[:, None] * frequency[None, :]
    sign = jnp.where(jnp.arange(head_dim) < half_width, -1.0, 1.0).astype(F32)
    tables = jnp.stack([jnp.cos(angles), jnp.sin(angles) * sign])
    outs = lax.switch(
        exponent, [partial(update, 1 << k, k) for k in range(LEVELS)],
        rate, norm_gain, tables, inputs, out_grad,
        w_qkv[0, 0], w_out[0, 0], mom_qkv[0, 0], mom_out[0, 0])
    return tuple(o[None, None] for o in outs)


def solution(mesh):
    return jax.shard_map(
        per_device,
        mesh=mesh,
        in_specs=(
            P("gossip", "fsdp", None),
            P("gossip", "fsdp", None),
            P("gossip", None),
            P("gossip", "fsdp", None, None),
            P("gossip", "fsdp", None, None),
            P("gossip", "fsdp", None, None),
            P("gossip", "fsdp", None, None),
            P(),
        ),
        out_specs=(
            P("gossip", "fsdp", None, None),
            P("gossip", "fsdp", None, None),
            P("gossip", "fsdp", None, None),
            P("gossip", "fsdp", None, None),
        ),
        check_vma=False,
    )
```

```python
from functools import partial
import math

import jax
import jax.numpy as jnp
from jax import lax
from jax.experimental import pallas as pl
from jax.experimental.pallas import tpu as pltpu
from jax.sharding import PartitionSpec as P

LEVELS = 3
BETA = 0.9
RATE = 0.1
EPSILON = 1e-05
FINE = 16
MESH = pl.DeviceIdType.MESH
F32 = jnp.float32
BF16 = jnp.bfloat16

(UP, UP_B, DOWN, DOWN_B, ACROSS, SIB, U2, D2, S_LO, S_HI, C_UP, C_DOWN, C_SIB, AX1, AX2, S_F1, S_F2,
 S_OLO, S_OHI, S_OF1, S_OF2) = range(21)
PER_ARRAY = 21
WQ = 2 * PER_ARRAY
WO = WQ + 1
MO = WQ + 2
WO2 = WQ + 3
MO2 = WQ + 4
MQ = WQ + 5


def dot_nt(a, b):
    return lax.dot_general(a, b, (((1,), (1,)), ((), ())), preferred_element_type=F32)


def dot_tn(a, b):
    return lax.dot_general(a, b, (((0,), (0,)), ((), ())), preferred_element_type=F32)


def pick(i, values):
    out = jnp.int32(values[0])
    for k in range(1, len(values)):
        out = jnp.where(i == k, jnp.int32(values[k]), out)
    return out


def average(own, other):
    return ((own.astype(F32) + other.astype(F32)) * 0.5).astype(BF16)


def move(weight, moved_m, rate):
    return (weight.astype(F32) - rate * moved_m.astype(F32)).astype(BF16)


def kernel(by, rate_ref, gain_ref, tab_ref,
           x_ref, og_ref, wq_ref, wo_ref, mq_ref, mo_ref,
           nwq_ref, nwo_ref, nmq_ref, nmo_ref,
           ax, aog, n_s, wrel, mrel, wq_v, wo_v, mq_v, mo_v, pq_v, po_v, rq_v, ro_v,
           lc_s, ls_s, q_s, k_s, v_s, qt_s, kt_s, vt_s, att_t, o_s, s_s, p_s, go_s, dk_s, dv_s, gp_s,
           send_sem, recv_sem, loc_sem):
    g = lax.axis_index("gossip")
    f = lax.axis_index("fsdp")
    n_g = lax.axis_size("gossip")
    core = lax.rem(f, 2)
    y = lax.rem(f // 2, 4)
    xh = f // 8
    chunks, block, width = ax.shape
    rows = block // 2
    half = rows // 2
    head_dim = wo_v.shape[0]
    out_scale = 1.0 / math.sqrt(lax.axis_size("fsdp") * head_dim)
    in_scale = 1.0 / math.sqrt(width)
    scale = 1.0 / math.sqrt(head_dim)

    def dev(xx, yy, cc):
        return xx * 8 + lax.rem(yy + 4, 4) * 2 + cc

    up = (g, dev(xh, y + 1, core))
    down = (g, dev(xh, y - 1, core))
    sib = (g, dev(xh, y, 1 - core))
    across = (g, dev(1 - xh, y, core))
    partner = (lax.rem(g + by, n_g), f)
    source = (lax.rem(g - by + n_g, n_g), f)
    leg = 6
    relayed = n_g - by == 2 * leg
    ahead = (lax.rem(g - leg + n_g, n_g), f)
    behind = (lax.rem(g + leg, n_g), f)
    along_y = by == 1

    def chunk(side, yy):
        return side * 4 + lax.rem(yy + 4, 4)

    def piece(dst, side, yy, part=None):
        first = pl.multiple_of(core * rows, rows)
        if part is None:
            return dst.at[chunk(side, yy), pl.ds(first, rows)]
        return dst.at[chunk(side, yy), pl.ds(pl.multiple_of(first + part * half, half), half)]

    def remote(i, src, dst, target):
        return pltpu.make_async_remote_copy(
            src_ref=src, dst_ref=dst, send_sem=send_sem.at[i], recv_sem=recv_sem.at[i],
            device_id=target, device_id_type=MESH)

    arrays = ((x_ref, ax), (og_ref, aog))

    def copy(a, i):
        src, dst = arrays[a]
        own, other = xh, 1 - xh
        n = a * PER_ARRAY + i

        def same(where, target):
            return remote(n, where, where, target)

        if i in (ACROSS, SIB):
            return remote(n, src.at[0], piece(dst, own, y), {ACROSS: across, SIB: sib}[i])
        if i in (UP, UP_B, DOWN, DOWN_B):
            part = 0 if i in (UP, DOWN_B) else 1
            return remote(n, src.at[0, pl.ds(part * half, half)], piece(dst, own, y, part),
                          up if i in (UP, UP_B) else down)
        if i == U2:
            return same(piece(dst, own, y - 1, 0), up)
        if i == D2:
            return same(piece(dst, own, y + 1, 1), down)
        if i == S_LO:
            return same(piece(dst, own, y - 1), sib)
        if i == S_HI:
            return same(piece(dst, own, y + 1), sib)
        if i in (C_UP, C_DOWN, C_SIB):
            return same(piece(dst, other, y), {C_UP: up, C_DOWN: down, C_SIB: sib}[i])
        if i == AX1:
            if along_y:
                return same(piece(dst, other, y - 1, 0), up)
            return same(piece(dst, own, y + 2, 0), across)
        if i == AX2:
            if along_y:
                return same(piece(dst, other, y + 1, 1), down)
            return same(piece(dst, own, y + 2, 1), across)
        if i == S_F1:
            return same(piece(dst, own, y + 2, 0), sib)
        if i == S_F2:
            return same(piece(dst, own, y + 2, 1), sib)
        if i == S_OLO:
            return same(piece(dst, other, y - 1), sib)
        if i == S_OHI:
            return same(piece(dst, other, y + 1), sib)
        if i == S_OF1:
            return same(piece(dst, other, y + 2, 0), sib)
        return same(piece(dst, other, y + 2, 1), sib)

    def start(a, *which):
        for i in which:
            copy(a, i).start()

    def arrived(a, *which):
        for i in which:
            copy(a, i).wait_recv()

    def local(i, src, dst):
        return pltpu.make_async_copy(src, dst, loc_sem.at[i])

    def own_copy(a):
        return local(a, arrays[a][0].at[0], piece(arrays[a][1], xh, y))

    loads = [local(2, wq_ref, wq_v), local(3, wo_ref, wo_v),
             local(4, mq_ref, mq_v), local(5, mo_ref, mo_v)]
    send_wq = remote(WQ, wq_ref, pq_v, partner)
    if relayed:
        send_wo = remote(WO, wo_ref, wrel, ahead)
        send_mo = remote(MO, mo_v, mrel, ahead)
        pass_wo = remote(WO2, wrel, po_v, ahead)
        pass_mo = remote(MO2, mrel, ro_v, ahead)
    else:
        send_wo = remote(WO, wo_ref, po_v, partner)
        send_mo = remote(MO, mo_v, ro_v, partner)

    def send_mq(d):
        at = pl.ds(pl.multiple_of(d * block, block), block)
        return remote(MQ + d, mq_v.at[at], rq_v.at[at], partner)

    own_copy(0).start()
    loads[0].start()
    barrier = pltpu.get_barrier_semaphore()
    everyone = [up, down, sib, across, partner, source]
    if relayed:
        everyone += [ahead, behind]
    for target in everyone:
        pl.semaphore_signal(barrier, inc=1, device_id=target, device_id_type=MESH)
    pl.semaphore_wait(barrier, len(everyone))
    start(0, UP, DOWN, UP_B, DOWN_B, ACROSS, SIB)
    if not along_y:
        send_wq.start()
        send_wo.start()
    own_copy(1).start()
    for c in loads[1:]:
        c.start()
    loads[0].wait()
    step = block // FINE
    fc, fs = tab_ref[0, pl.ds(chunks + FINE, step), :], tab_ref[1, pl.ds(chunks + FINE, step), :]
    for c in range(FINE):
        at = pl.ds(c * step, step)
        cc, cs = tab_ref[0, pl.ds(chunks + c, 1), :], tab_ref[1, pl.ds(chunks + c, 1), :]
        lc_s[at, :] = cc * fc - cs * fs
        ls_s[at, :] = cs * fc + cc * fs

    def near(a):
        arrived(a, UP)
        start(a, U2)
        arrived(a, DOWN)
        start(a, D2)

    def near_rest(a):
        arrived(a, UP_B)
        start(a, S_LO)
        arrived(a, DOWN_B)
        start(a, S_HI)

    def row(a):
        if a == 0 or not along_y:
            arrived(a, ACROSS)
        start(a, C_UP, C_DOWN, C_SIB)
        if a == 0 and along_y:
            start(1, ACROSS)

    def far(a):
        arrived(a, U2)
        start(a, *((S_F1,) if along_y else (AX1, S_F1)))
        arrived(a, D2)
        start(a, *((S_F2,) if along_y else (AX2, S_F2)))

    def other_near(a):
        arrived(a, C_UP)
        start(a, *((AX1, S_OLO) if along_y else (S_OLO,)))
        arrived(a, C_DOWN)
        start(a, *((AX2, S_OHI) if along_y else (S_OHI,)))

    def other_far(a):
        arrived(a, AX1)
        start(a, S_OF1)
        arrived(a, AX2)
        start(a, S_OF2)

    def second_array(late):
        if along_y and late:
            arrived(1, ACROSS)
            send_wq.start()
            send_wo.start()
        if late == along_y:
            start(1, UP, DOWN, UP_B, DOWN_B, *((SIB,) if along_y else (ACROSS, SIB)))

    def when(i, k, *steps):
        @pl.when(i == k)
        def _():
            for s in steps:
                s()

    def chunk_at(i):
        side = pick(i, (0, 0, 0, 1, 0, 1, 1, 1))
        move_y = pick(i, (0, 3, 1, 0, 2, 3, 1, 2))
        return lax.rem(xh + side, 2) * 4 + lax.rem(y + move_y, 4)

    def tables(m):
        hc, hs = tab_ref[0, pl.ds(m, 1), :], tab_ref[1, pl.ds(m, 1), :]
        lc, ls = lc_s[...], ls_s[...]
        return hc * lc - hs * ls, hs * lc + hc * ls

    def turned(t):
        return pltpu.roll(t, head_dim // 2, 1)

    def project(i, _):
        when(i, 0, lambda: own_copy(0).wait(), lambda: arrived(0, SIB),
             lambda: near(0))
        when(i, 1, lambda: near_rest(0), lambda: row(0), lambda: arrived(0, S_LO))
        when(i, 2, lambda: arrived(0, S_HI))
        when(i, 3, lambda: far(0), lambda: second_array(False), lambda: arrived(0, C_SIB))
        when(i, 4, lambda: arrived(0, S_F1, S_F2))
        when(i, 5, lambda: other_near(0), lambda: second_array(True), lambda: arrived(0, S_OLO))
        when(i, 7 if along_y else 6, lambda: other_far(0))
        when(i, 6, lambda: arrived(0, S_OHI))
        when(i, 7, lambda: arrived(0, S_OF1, S_OF2))
        m = chunk_at(i)

        columns = [slice(c, c + head_dim) for c in range(0, width, head_dim)]
        squares = jnp.zeros((block, head_dim), F32)
        for at in columns:
            t = ax[m, :, at].astype(F32)
            squares = squares + t * t
        stats = lax.rsqrt(jnp.sum(squares, -1, keepdims=True) * (1.0 / width) + EPSILON)
        for at in columns:
            n_s[m, :, at] = (ax[m, :, at].astype(F32) * stats * gain_ref[:, at]).astype(BF16)
        proj = jnp.dot(n_s[m], wq_v[...], preferred_element_type=F32) * in_scale
        cos, sin = tables(m)
        q = proj[:, :head_dim]
        k = proj[:, head_dim:2 * head_dim]
        q = (q * cos + turned(q) * sin).astype(BF16)
        k = (k * cos + turned(k) * sin).astype(BF16)
        v = proj[:, 2 * head_dim:].astype(BF16)
        q_s[m], k_s[m], v_s[m] = q, k, v
        qt_s[m], kt_s[m], vt_s[m] = q.T, k.T, v.T
        dk_s[m] = jnp.zeros_like(dk_s[m])
        dv_s[m] = jnp.zeros_like(dv_s[m])
        return 0

    lax.fori_loop(0, chunks, project, 0)

    row_pos = lax.broadcasted_iota(jnp.int32, (block, block), 0)
    col_pos = lax.broadcasted_iota(jnp.int32, (block, block), 1)

    def folded(t, op):
        return op(t.reshape(block // 8, 8, block), axis=0)

    def forward(m, _):
        if relayed:
            when(m, 1, send_wo.wait_recv, pass_wo.start)
        when(m, 4 if along_y else 0, lambda: near(1))
        when(m, 7 if along_y else 5, lambda: near_rest(1), lambda: row(1))
        if not along_y:
            when(m, 7, lambda: far(1))
        queries = qt_s[m]

        def scores(j, top):
            for u in (2 * j, 2 * j + 1):
                s = jnp.dot(k_s[u], queries, preferred_element_type=F32) * scale
                s = jnp.where(row_pos + u * block <= col_pos + m * block, s, -jnp.inf)
                s_s[u] = s
                top = jnp.maximum(top, folded(s, jnp.max))
            return top

        top = lax.fori_loop(0, (m + 2) // 2, scores, jnp.full((8, block), -jnp.inf, F32))
        top = jnp.max(top, 0, keepdims=True)

        def exps(j, total):
            for u in (2 * j, 2 * j + 1):
                e = jnp.exp(s_s[u] - top)
                s_s[u] = e
                total = total + folded(e, jnp.sum)
            return total

        total = lax.fori_loop(0, (m + 2) // 2, exps, jnp.zeros((8, block), F32))
        inverse = 1.0 / jnp.sum(total, 0, keepdims=True)

        def values(j, out):
            for u in (2 * j, 2 * j + 1):
                p = (s_s[u] * inverse).astype(BF16)
                p_s[m, u] = p
                out = out + jnp.dot(vt_s[u], p, preferred_element_type=F32)
            return out

        out = lax.fori_loop(0, (m + 2) // 2, values, jnp.zeros((head_dim, block), F32))
        o_s[m] = out
        att_t[m] = out.astype(BF16)
        return 0

    lax.fori_loop(0, chunks, forward, 0)
    for c in loads[1:]:
        c.wait()
    go_s[...] = jnp.zeros_like(go_s)

    def backward(i, _):
        when(i, 0, lambda: own_copy(1).wait(), lambda: arrived(1, SIB))
        when(i, 1, lambda: arrived(1, S_LO))
        when(i, 2, lambda: arrived(1, S_HI))
        if along_y:
            when(i, 3, lambda: far(1))
        when(i, 3, lambda: arrived(1, C_SIB))
        when(i, 5 if along_y else 4, lambda: other_near(1))
        when(i, 4, lambda: arrived(1, S_F1, S_F2))
        when(i, 5, lambda: arrived(1, S_OLO))
        when(i, 7 if along_y else 6, lambda: other_far(1))
        when(i, 6, lambda: arrived(1, S_OHI))
        when(i, 7, lambda: arrived(1, S_OF1, S_OF2))
        m = chunk_at(i)
        da = (dot_nt(aog[m], wo_v[...]) * out_scale).astype(BF16)
        da_t = da.T
        go_s[...] += jnp.dot(att_t[m], aog[m], preferred_element_type=F32)

        @pl.when(i == chunks - 1)
        def _():
            def moved(r, _):
                at = pl.ds(pl.multiple_of(r * 16, 16), 16)
                grad = (go_s[at, :] * out_scale).astype(BF16)
                mo_v[at, :] = (BETA * mo_v[at, :].astype(F32) + grad.astype(F32)).astype(BF16)
                return 0

            lax.fori_loop(0, head_dim // 16, moved, 0)
            send_mo.start()

        centre = jnp.sum(da_t.astype(F32) * o_s[m], 0, keepdims=True)
        q = q_s[m]

        def pair(j, dq):
            for u in (2 * j, 2 * j + 1):
                p = p_s[m, u]
                dp = jnp.dot(v_s[u], da_t, preferred_element_type=F32)
                ds = (p.astype(F32) * (dp - centre) * scale).astype(BF16)
                dk_s[u] += jnp.dot(ds, q, preferred_element_type=F32)
                dv_s[u] += jnp.dot(p, da, preferred_element_type=F32)
                dq = dq + jnp.dot(kt_s[u], ds, preferred_element_type=F32)
            return dq

        dq = lax.fori_loop(0, (m + 2) // 2, pair, jnp.zeros((head_dim, block), F32)).T
        cos, sin = tables(m)
        gp_s[m, :, :head_dim] = ((dq * cos - turned(dq) * sin) * in_scale).astype(BF16)
        return 0

    lax.fori_loop(0, chunks, backward, 0)

    def finish(m, _):
        cos, sin = tables(m)
        dk = dk_s[m]
        gp_s[m, :, head_dim:2 * head_dim] = (
            (dk * cos - turned(dk) * sin) * in_scale).astype(BF16)
        gp_s[m, :, 2 * head_dim:] = (dv_s[m] * in_scale).astype(BF16)
        return 0

    lax.fori_loop(0, chunks, finish, 0)

    def grads(d, _):
        at = pl.ds(pl.multiple_of(d * block, block), block)
        total = dot_tn(n_s[0, :, at], gp_s[0])
        for m in range(1, chunks):
            total = total + dot_tn(n_s[m, :, at], gp_s[m])
        mq_v[at, :] = (BETA * mq_v[at, :].astype(F32)
                       + total.astype(BF16).astype(F32)).astype(BF16)
        send_mq(d).start()
        return 0

    lax.fori_loop(0, width // block, grads, 0)
    rate = rate_ref[0]
    send_wq.wait()
    if relayed:
        send_wo.wait_send()
        pass_wo.wait()
        send_mo.wait()
        pass_mo.start()
    else:
        send_wo.wait()
        send_mo.wait()

    def outs_o(r, _):
        at = pl.ds(pl.multiple_of(r * 16, 16), 16)
        mine, theirs = mo_v[at, :], ro_v[at, :]
        nmo_ref[at, :] = average(mine, theirs)
        nwo_ref[at, :] = average(move(wo_v[at, :], mine, rate), move(po_v[at, :], theirs, rate))
        return 0

    if not relayed:
        lax.fori_loop(0, head_dim // 16, outs_o, 0)

    def outs_q(d, _):
        send_mq(d).wait()
        at = pl.ds(pl.multiple_of(d * block, block), block)
        mine, theirs = mq_v[at, :], rq_v[at, :]
        nmq_ref[at, :] = average(mine, theirs)
        nwq_ref[at, :] = average(move(wq_v[at, :], mine, rate), move(pq_v[at, :], theirs, rate))
        return 0

    lax.fori_loop(0, width // block, outs_q, 0)
    if relayed:
        pass_mo.wait()
        lax.fori_loop(0, head_dim // 16, outs_o, 0)

    for a in range(2):
        for i in range(PER_ARRAY):
            copy(a, i).wait_send()


def update(by, cid, rate, gain, tables, x, og, wq, wo, mq, mo):
    devices = lax.axis_size("fsdp")
    rows, width = x.shape[1:]
    block = 2 * rows
    chunks = devices // 2
    wide, head_dim = wq.shape[1], wo.shape[0]
    hbm = pl.BlockSpec(memory_space=pl.ANY)
    vmem = pl.BlockSpec(memory_space=pltpu.VMEM)
    n_copies = MQ + width // block

    def v(*shape, dtype=BF16):
        return pltpu.VMEM(shape, dtype)

    return pl.pallas_call(
        partial(kernel, by),
        out_shape=(
            jax.ShapeDtypeStruct(wq.shape, BF16), jax.ShapeDtypeStruct(wo.shape, BF16),
            jax.ShapeDtypeStruct(wq.shape, BF16), jax.ShapeDtypeStruct(wo.shape, BF16),
        ),
        in_specs=[pl.BlockSpec(memory_space=pltpu.SMEM)] + [vmem] * 2 + [hbm] * 6,
        out_specs=[vmem] * 4,
        scratch_shapes=[
            v(chunks, block, width), v(chunks, block, width), v(chunks, block, width),
            v(head_dim, width), v(head_dim, width),
            v(width, wide), v(head_dim, width), v(width, wide), v(head_dim, width),
            v(width, wide), v(head_dim, width), v(width, wide), v(head_dim, width),
            v(block, head_dim, dtype=F32), v(block, head_dim, dtype=F32),
            v(chunks, block, head_dim), v(chunks, block, head_dim), v(chunks, block, head_dim),
            v(chunks, head_dim, block), v(chunks, head_dim, block), v(chunks, head_dim, block),
            v(chunks, head_dim, block), v(chunks, head_dim, block, dtype=F32),
            v(chunks, block, block, dtype=F32), v(chunks, chunks, block, block),
            v(head_dim, width, dtype=F32),
            v(chunks, block, head_dim, dtype=F32), v(chunks, block, head_dim, dtype=F32),
            v(chunks, block, wide),
            pltpu.SemaphoreType.DMA((n_copies,)), pltpu.SemaphoreType.DMA((n_copies,)),
            pltpu.SemaphoreType.DMA((6,)),
        ],
        name=f"update_{by}",
        compiler_params=pltpu.CompilerParams(
            collective_id=cid, has_side_effects=True, vmem_limit_bytes=66_000_000),
    )(rate, gain, tables, x, og, wq, wo, mq, mo)


def per_device(inputs, out_grad, norm_gain, w_qkv, w_out, mom_qkv, mom_out, step_index):
    rate = RATE * (step_index.astype(F32) + 1.0) / (4.0 * LEVELS)
    exponent = jnp.remainder(step_index[0], LEVELS)
    head_dim = w_out.shape[2]
    rows = inputs.shape[1]
    block, chunks = 2 * rows, lax.axis_size("fsdp") // 2
    half_width = head_dim // 2
    frequency = jnp.exp(
        -math.log(10000.0) * 2.0 * jnp.arange(half_width, dtype=F32) / head_dim)
    frequency = jnp.concatenate([frequency, frequency])
    step = block // FINE
    positions = jnp.concatenate(
        [jnp.arange(chunks) * block, jnp.arange(FINE) * step, jnp.arange(step)])
    angles = positions.astype(F32)[:, None] * frequency[None, :]
    sign = jnp.where(jnp.arange(head_dim) < half_width, -1.0, 1.0).astype(F32)
    tables = jnp.stack([jnp.cos(angles), jnp.sin(angles) * sign])
    outs = lax.switch(
        exponent, [partial(update, 1 << k, k) for k in range(LEVELS)],
        rate, norm_gain, tables, inputs, out_grad,
        w_qkv[0, 0], w_out[0, 0], mom_qkv[0, 0], mom_out[0, 0])
    return tuple(o[None, None] for o in outs)


def solution(mesh):
    return jax.shard_map(
        per_device,
        mesh=mesh,
        in_specs=(
            P("gossip", "fsdp", None),
            P("gossip", "fsdp", None),
            P("gossip", None),
            P("gossip", "fsdp", None, None),
            P("gossip", "fsdp", None, None),
            P("gossip", "fsdp", None, None),
            P("gossip", "fsdp", None, None),
            P(),
        ),
        out_specs=(
            P("gossip", "fsdp", None, None),
            P("gossip", "fsdp", None, None),
            P("gossip", "fsdp", None, None),
            P("gossip", "fsdp", None, None),
        ),
        check_vma=False,
    )
```
